512 devices in a mesh: dom: 64 (over z_hi, x, y, core), grp: 8 (over z_lo).
Axes of the slice: x: 4, y: 4, z: 16 (z_hi: 2, z_lo: 8; z = z_hi * 8 + z_lo), core: 2. Of those that a mesh axis runs over, the one named last changes fastest.
Arguments:
- features: bfloat16 [4096, 768], P(('dom', 'grp')), may hold values from -6 to 6
- w_first: bfloat16 [768, 512], replicated, may hold values from -0.21875 to 0.21875
- w_second: bfloat16 [512, 512], replicated, may hold values from -0.25 to 0.25
- relation_table: bfloat16 [1387, 512], replicated, may hold values from -1.5 to 1.5
- heads: int32 [2, 65536], P(None, ('dom', 'grp')), may hold values from 0 to 63
- relations: int32 [2, 65536], P(None, ('dom', 'grp')), may hold values from 0 to 1386
- tails: int32 [2, 65536], P(None, ('dom', 'grp')), may hold values from 0 to 63
- negatives: int32 [2, 512], replicated, may hold values from 0 to 63
- partner: int32 [2, 64], replicated, may hold values from 0 to 63, as said below
Outputs:
- edge_loss: float32 [2, 65536], P(None, ('dom', 'grp'))
- grad_w1: float32 [768, 512], P('grp')
- grad_w2: float32 [512, 512], P('grp')
The draws below stay inside these ranges and needn't reach their ends.
Inputs may be any that keep to these rules, and one draw needn't show every extreme that they name: partner[r, p] = p XOR m_r with one mask m_r of 1 to 63 for each round r, so partitions meet in pairs.
All inputs are finite; a program needn't handle non-finite values.
Results may differ from the reference program's by a relative error of at most 0.0095.
Values may be sent and summed in bfloat16 or wider, within the bound.
A program may use at most 64 MiB of HBM per device.

```python
import math
import jax
import jax.numpy as jnp
import numpy as np
from jax import lax

D_IN = 768
NREL = 1387
D_HID = 512
D_ENC = 512
NEG = 512
ROUNDS = 2
EDGE_DEV = 128
NPART = 64
GROUP = 8
ENT_PART = 64
ENTITIES = 4096
EDGES = 65536


def draw_partner(key, part):
    masks = jax.random.randint(jax.random.fold_in(key, 7), (ROUNDS, 1), 1, NPART)
    base = jnp.arange(NPART, dtype=jnp.int32)[None, :]
    return jnp.bitwise_xor(base, masks.astype(jnp.int32)).astype(jnp.int32)


def plant(values, rng, low, top_value):
    longest = values.shape.index(max(values.shape))
    spots = []
    for shift in (0, 1):
        where = [jax.random.randint(jax.random.fold_in(rng, axis), (), 0, length) for axis, length in enumerate(values.shape)]
        where[longest] = (where[longest] + shift) % values.shape[longest]
        spots.append(tuple(where))
    return values.at[spots[0]].set(low).at[spots[1]].set(top_value)


def levels(rng, extent, pieces, smallest, high):
    def one(position, parts):
        heights = jax.random.uniform(jax.random.fold_in(jax.random.fold_in(rng, 6), position), (parts,), jnp.float32, smallest / len(pieces), high / len(pieces))
        return jnp.repeat(jnp.exp(heights), extent[position] // parts).reshape((-1,) + (1,) * (len(extent) - position - 1))

    gain = one(*pieces[0])
    for cut in pieces[1:]:
        gain = gain * one(*cut)
    return gain


def rank_table(amount, lean):
    loads = [(1 << 20) // math.isqrt(standing ** lean) + 1 for standing in range(1, amount + 1)]
    width = 1 + sum(loads) // (1 << 30)
    return np.cumsum(np.array([max(1, weight // width) for weight in loads]))


def skewed_ids(key, dims, count, slope):
    grid = rank_table(count, slope)
    ticket = jax.random.randint(jax.random.fold_in(key, 1), dims, 0, int(grid[count - 1]))
    standing = jnp.searchsorted(jnp.asarray(grid, jnp.int32), ticket, side="right")
    return jax.random.permutation(jax.random.fold_in(key, 2), count)[standing].astype(jnp.int32)


def gaussian(rng, shape, deviation, limit, split=(), kind=jnp.bfloat16):
    entries = jax.random.normal(rng, shape, jnp.float32) * deviation
    if len(split) > 0:
        entries = levels(rng, shape, split, -0.22, 0.18) * entries
    return jnp.clip(entries, min=-limit, max=limit).astype(kind)


def setup_inputs(seed: int = 0) -> dict:
    splits = jax.random.split(jax.random.key(seed), 10)
    return {
        "features": gaussian(splits[0], (ENTITIES, D_IN), 1.0, 6.0, ((0, 512),)),
        "w_first": gaussian(splits[1], (D_IN, D_HID), D_IN ** -0.5, 0.21875),
        "w_second": gaussian(splits[2], (D_HID, D_ENC), D_HID ** -0.5, 0.25),
        "relation_table": gaussian(splits[3], (NREL, D_ENC), 0.25, 1.5),
        "heads": plant(jax.random.randint(splits[4], (ROUNDS, EDGES), 0, ENT_PART), jax.random.fold_in(splits[4], 1), 0, ENT_PART - 1).astype(jnp.int32),
        "relations": plant(skewed_ids(splits[5], (ROUNDS, EDGES), NREL, 2), jax.random.fold_in(splits[5], 3), 0, NREL - 1).astype(jnp.int32),
        "tails": plant(jax.random.randint(splits[6], (ROUNDS, EDGES), 0, ENT_PART), jax.random.fold_in(splits[6], 1), 0, ENT_PART - 1).astype(jnp.int32),
        "negatives": plant(jax.random.randint(splits[7], (ROUNDS, NEG), 0, ENT_PART), jax.random.fold_in(splits[7], 1), 0, ENT_PART - 1).astype(jnp.int32),
        "partner": draw_partner(jax.random.fold_in(splits[9], 71), 0),
    }


def encode(rows, w_first, w_second):
    pre_act = jnp.dot(rows, w_first, preferred_element_type=jnp.float32)
    hidden = jax.nn.silu(pre_act).astype(jnp.bfloat16)
    encoded = jnp.dot(hidden, w_second, preferred_element_type=jnp.float32).astype(jnp.bfloat16)
    return (pre_act, hidden, encoded)

def backward(rows, pre_act, hidden, grad_rows, w_second):
    term_second = lax.dot_general(hidden, grad_rows, (((0,), (0,)), ((), ())), preferred_element_type=jnp.float32)
    grad_hidden = lax.dot_general(grad_rows, w_second, (((1,), (1,)), ((), ())), preferred_element_type=jnp.float32)
    sigmoid_pre = jax.nn.sigmoid(pre_act)
    silu_slope = sigmoid_pre * (1.0 + pre_act * (1.0 - sigmoid_pre))
    grad_pre = (grad_hidden * silu_slope).astype(jnp.bfloat16)
    term_first = lax.dot_general(rows, grad_pre, (((0,), (0,)), ((), ())), preferred_element_type=jnp.float32)
    return (term_first, term_second)

def score_block(own, other, relation_table, head_ids, relation_ids, tail_ids, negative_ids):
    half_width = own.shape[1] // 2
    head_rows = jnp.take(own, head_ids, axis=0).astype(jnp.float32)
    rel_rows = jnp.take(relation_table, relation_ids, axis=0).astype(jnp.float32)
    tail_rows = jnp.take(other, tail_ids, axis=0).astype(jnp.float32)
    negative_rows = jnp.take(other, negative_ids, axis=0)
    head_real, head_imag = (head_rows[:, :half_width], head_rows[:, half_width:])
    rel_real, rel_imag = (rel_rows[:, :half_width], rel_rows[:, half_width:])
    query = jnp.concatenate([head_real * rel_real - head_imag * rel_imag, head_real * rel_imag + head_imag * rel_real], axis=1).astype(jnp.bfloat16)
    query_wide = query.astype(jnp.float32)
    positive = lax.optimization_barrier(jnp.sum(query_wide * tail_rows, axis=1))
    negative = lax.dot_general(query, negative_rows, (((1,), (1,)), ((), ())), preferred_element_type=jnp.float32)
    edge_loss = jax.nn.softplus(-positive) + lax.optimization_barrier(jnp.sum(jax.nn.softplus(negative), axis=1)) / negative.shape[1]
    weight_neg = (jax.nn.sigmoid(negative) / negative.shape[1]).astype(jnp.bfloat16)
    weight_pos = -jax.nn.sigmoid(-positive)
    grad_query = weight_pos[:, None] * tail_rows + jnp.dot(weight_neg, negative_rows, preferred_element_type=jnp.float32)
    grad_tail = weight_pos[:, None] * query_wide
    grad_negative = lax.dot_general(weight_neg, query, (((0,), (0,)), ((), ())), preferred_element_type=jnp.float32)
    grad_real, grad_imag = (grad_query[:, :half_width], grad_query[:, half_width:])
    grad_head = jnp.concatenate([grad_real * rel_real + grad_imag * rel_imag, grad_imag * rel_real - grad_real * rel_imag], axis=1)
    row_count = own.shape[0]
    own_part = jax.ops.segment_sum(grad_head, head_ids, num_segments=row_count)
    far_part = jax.ops.segment_sum(grad_tail, tail_ids, num_segments=row_count) + jax.ops.segment_sum(grad_negative, negative_ids, num_segments=row_count)
    return (edge_loss, own_part, far_part)

def take_rows(table, part_index, row_count):
    start = (part_index * row_count).astype(jnp.int32)
    return lax.dynamic_slice_in_dim(table, start, row_count, 0)

def group_total(partials):
    narrow = lax.optimization_barrier(partials.astype(jnp.bfloat16))
    return lax.optimization_barrier(jnp.sum(narrow.astype(jnp.float32), axis=0)).astype(jnp.bfloat16)

def reference(features, w_first, w_second, relation_table, heads, relations, tails, negatives, partner):
    pre_act, hidden, encoded = encode(features, w_first, w_second)
    part_count = partner.shape[1]
    row_count = encoded.shape[0] // part_count
    edge_span = heads.shape[1] // part_count
    zero_first = jnp.zeros(w_first.shape, jnp.float32)
    zero_second = jnp.zeros(w_second.shape, jnp.float32)

    def one_partition(totals, part_index):
        total_first, total_second = totals
        own = take_rows(encoded, part_index, row_count)
        own_acc = jnp.zeros((GROUP, row_count, encoded.shape[1]), jnp.float32)
        round_losses = []
        for bucket in range(ROUNDS):
            partner_index = partner[bucket, part_index]
            other = take_rows(encoded, partner_index, row_count)

            def member_ids(table):
                return take_rows(table[bucket], part_index, edge_span).reshape(GROUP, EDGE_DEV)

            def member(edge_tuple):
                return score_block(own, other, relation_table, edge_tuple[0], edge_tuple[1], edge_tuple[2], negatives[bucket])
            edge_loss, own_part, far_part = lax.map(member, (member_ids(heads), member_ids(relations), member_ids(tails)))
            round_losses.append(edge_loss.reshape(edge_span))
            own_acc = own_acc + own_part
            far_grad = group_total(far_part)
            term_first, term_second = backward(take_rows(features, partner_index, row_count), take_rows(pre_act, partner_index, row_count), take_rows(hidden, partner_index, row_count), far_grad, w_second)
            total_first = total_first + term_first
            total_second = total_second + term_second
        own_grad = group_total(own_acc)
        term_first, term_second = backward(take_rows(features, part_index, row_count), take_rows(pre_act, part_index, row_count), take_rows(hidden, part_index, row_count), own_grad, w_second)
        return ((total_first + term_first, total_second + term_second), jnp.stack(round_losses))
    totals, losses = lax.scan(one_partition, (zero_first, zero_second), jnp.arange(part_count, dtype=jnp.int32))
    total_first, total_second = totals
    edge_loss = jnp.transpose(losses, (1, 0, 2)).reshape(ROUNDS, heads.shape[1])
    squares = jnp.sum(total_first * total_first) + jnp.sum(total_second * total_second)
    factor = jnp.minimum(1.0, math.sqrt(w_first.size + w_second.size) / jnp.sqrt(squares + 1e-06))
    return (edge_loss, total_first * factor, total_second * factor)
```

```python
import functools
import math

import jax
import jax.numpy as jnp
from jax import lax
from jax.experimental import pallas as pl
from jax.experimental.pallas import tpu as pltpu
from jax.sharding import PartitionSpec as P

MESH = pl.DeviceIdType.MESH
BF = jnp.bfloat16
F32 = jnp.float32
HOP = 3


def mm(a, b):
    return jnp.dot(a, b, preferred_element_type=F32)


def nt(a, b):
    return lax.dot_general(a, b, (((1,), (1,)), ((), ())), preferred_element_type=F32)


def tn(a, b):
    return lax.dot_general(a, b, (((0,), (0,)), ((), ())), preferred_element_type=F32)


def sigmoid(v):
    return 1.0 / (1.0 + jnp.exp(-v))


def softplus(v):
    return jnp.maximum(v, 0.0) + jnp.log1p(jnp.exp(-jnp.abs(v)))


def body(
    dims,
    feat,
    w1_hbm,
    w2_hbm,
    table_hbm,
    heads,
    rels,
    tails,
    negs,
    partner,
    loss_out,
    g1_out,
    g2_out,
    w1,
    w2,
    table,
    ids,
    buf_y,
    send_x,
    buf_x,
    buf_z,
    buf_o,
    rel_rows,
    query,
    enc,
    slope,
    grads,
    dpre,
    xt,
    ht,
    core_send,
    core_recv,
    total,
    send_1,
    recv_1,
    part_2,
    send_2,
    recv_2,
    send_z,
    recv_z,
    gathered,
    squares,
    load_sem,
    send_sem,
    sem_y,
    sem_x,
    sem_z,
    sem_o,
    sem_core,
    sem_1,
    sem_2,
    sem_rz,
    sem_b,
    sem_a,
    sem_g,
    sem_s,
):
    nzh, na, ng = dims
    nz = nzh * ng
    rem, div = lax.rem, lax.div
    dom = lax.axis_index("dom")
    g = lax.axis_index("grp")
    c = rem(dom, 2)
    y = rem(div(dom, 2), na)
    x = rem(div(dom, 2 * na), na)
    zh = div(dom, 2 * na * na)
    z = zh * ng + g
    bits = na.bit_length() - 1

    def dev(zh_, x_, y_, c_, g_):
        return (((zh_ * na + x_) * na + y_) * 2 + c_, g_)

    def xor(v, k):
        out = 0
        for b in range(bits):
            out = out + rem(div(v, 1 << b) + (k >> b & 1), 2) * (1 << b)
        return out

    def on_ring(step):
        to = rem(z + step + nz, nz)
        return dev(div(to, ng), x, y, c, rem(to, ng))

    other_core = dev(zh, x, y, 1 - c, g)
    pending = []
    counter = [0]

    def push(src, dst, sem, target, keep=True):
        copy = pltpu.make_async_remote_copy(
            src_ref=src,
            dst_ref=dst,
            send_sem=send_sem.at[counter[0]],
            recv_sem=sem,
            device_id=target,
            device_id_type=MESH,
        )
        counter[0] += 1
        copy.start()
        if keep:
            pending.append(copy)
        return copy

    def arrived(dst, sem):
        pltpu.make_async_remote_copy(
            src_ref=dst,
            dst_ref=dst,
            send_sem=send_sem.at[0],
            recv_sem=sem,
            device_id=other_core,
            device_id_type=MESH,
        ).wait_recv()

    barrier = pltpu.get_barrier_semaphore()
    peers = [
        dev(zh, x, xor(y, k >> 1), rem(c + (k & 1), 2), g) for k in range(1, 2 * na)
    ]
    peers += [dev(zh, xor(x, k), y, c, g) for k in range(1, na)]
    peers += [on_ring(k) for k in range(1, nz)]
    peers += [dev(zh, x, y, 1 - c, rem(g + k, ng)) for k in range(1, ng)]
    for peer in peers:
        pl.semaphore_signal(barrier, inc=1, device_id=peer, device_id_type=MESH)

    loads = [
        pltpu.make_async_copy(table_hbm, table, load_sem.at[0]),
        pltpu.make_async_copy(w1_hbm, w1, load_sem.at[1]),
        pltpu.make_async_copy(w2_hbm, w2, load_sem.at[2]),
    ]
    for load in loads:
        load.start()
    buf_y[0] = feat[...]
    buf_o[g] = feat[...]
    ids[0:2] = heads[...].astype(F32)
    ids[2:4] = rels[...].astype(F32)
    ids[4:6] = tails[...].astype(F32)
    ids[6:8] = jnp.zeros_like(ids[6:8])
    pl.semaphore_wait(barrier, len(peers))

    for k in range(1, 2 * na):
        push(feat, buf_y.at[k], sem_y.at[k], dev(zh, x, xor(y, k >> 1), rem(c + (k & 1), 2), g))
    for k in range(1, ng):
        push(feat, buf_o.at[g], sem_o.at[g], dev(zh, x, y, c, rem(g + k, ng)))

    columns = jnp.transpose(ids[...])
    loads[0].wait()
    nrel = table.shape[0]
    edges = heads.shape[1]
    for r in range(2):
        pick = lax.broadcasted_iota(jnp.int32, (edges, nrel), 1).astype(F32) == columns[:, 2 + r : 3 + r]
        rel_rows[r] = mm(pick.astype(BF), table[...]).astype(BF)

    masks = [partner[r, 0] for r in range(2)]
    for k in range(1, 2 * na):
        arrived(buf_y.at[k], sem_y.at[k])
    for r in range(2):
        send_x[r] = buf_y[masks[r] % (2 * na)]
    for k in range(1, na):
        push(send_x, buf_x.at[k], sem_x.at[k], dev(zh, xor(x, k), y, c, g))
    buf_x[0] = send_x[...]
    for k in range(1, na):
        arrived(buf_x.at[k], sem_x.at[k])
    for r in range(2):
        buf_z[z, r] = buf_x[(masks[r] // (2 * na)) % na, r]

    reach = {1: nz // 2, -1: nz - 1 - nz // 2}
    seen = set()
    level = 0
    while HOP * level < reach[1]:
        for way in (1, -1):
            base = HOP * level
            if base >= reach[way]:
                continue
            source = rem(z - way * base + nz, nz)
            if level:
                arrived(buf_z.at[source], sem_z.at[source])
                seen.add(-way * base)
            for step in range(1, HOP + 1):
                if base + step <= reach[way]:
                    push(buf_z.at[source], buf_z.at[source], sem_z.at[source], on_ring(way * step))
        if level == 0:
            loads[1].wait()
            loads[2].wait()
            for k in range(1, ng):
                src = rem(g + k, ng)
                arrived(buf_o.at[src], sem_o.at[src])
            rows = 8 * ng
            half = w2.shape[1] // 2
            lane = lax.broadcasted_iota(jnp.int32, (edges, rows), 1).astype(F32)

            def encode(x_rows, first, count, at):
                pre = mm(x_rows, w1[...])
                s = sigmoid(pre)
                hidden = (pre * s).astype(BF)
                enc[first : first + count] = mm(hidden, w2[...]).astype(BF)
                slope[first : first + count] = s * (1.0 + pre * (1.0 - s))
                xt[:, at : at + count] = jnp.transpose(x_rows)
                ht[:, at : at + count] = jnp.transpose(hidden)

            own_x = buf_o[...].astype(F32).reshape(rows, feat.shape[1]).astype(BF)
            encode(own_x, 2 * rows, rows, 2 * rows)
            picks = []
            for r in range(2):
                head_pick = (lane == columns[:, r : r + 1]).astype(BF)
                picks.append(head_pick)
                head = mm(head_pick, enc[2 * rows : 3 * rows])
                rel = rel_rows[r].astype(F32)
                h_re, h_im = head[:, :half], head[:, half:]
                r_re, r_im = rel[:, :half], rel[:, half:]
                query[r, :, :half] = (h_re * r_re - h_im * r_im).astype(BF)
                query[r, :, half:] = (h_re * r_im + h_im * r_re).astype(BF)
            counts = []
            nneg = negs.shape[1]
            for r in range(2):
                hit = lax.broadcasted_iota(jnp.int32, (rows, nneg), 0) == negs[r : r + 1, :]
                counts.append(nt(jnp.ones((8, nneg), BF), hit.astype(F32).astype(BF))[0:1])
        level += 1
    for way in (1, -1):
        for dist in range(1, reach[way] + 1):
            if -way * dist not in seen:
                source = rem(z - way * dist + nz, nz)
                arrived(buf_z.at[source], sem_z.at[source])

    far = []
    for r in range(2):
        half_of = rem(zh + (masks[r] // (2 * na * na)) % 2, 2)
        rows_r = buf_z[pl.ds(half_of * ng, ng), r]
        far.append(rows_r.astype(F32).reshape(rows, feat.shape[1]))
    encode(jnp.concatenate(far, axis=0).astype(BF), 0, 2 * rows, 0)

    own = None
    losses = []
    for r in range(2):
        other = enc[r * rows : (r + 1) * rows]
        q = query[r]
        score = nt(q, other)
        tail_pick = jnp.where(lane == columns[:, 4 + r : 5 + r], 1.0, 0.0)
        positive = jnp.sum(score * tail_pick, axis=1, keepdims=True)
        losses.append(
            softplus(-positive) + jnp.sum(softplus(score) * counts[r], axis=1, keepdims=True) / nneg
        )
        weight_neg = (sigmoid(score) / nneg).astype(BF).astype(F32)
        weight_pos = -sigmoid(-positive)
        weight = (weight_neg * counts[r] + tail_pick * weight_pos).astype(BF)
        d_query = mm(weight, other)
        grads[r * rows : (r + 1) * rows] = tn(weight, q).astype(BF)
        rel = rel_rows[r].astype(F32)
        q_re, q_im = d_query[:, :half], d_query[:, half:]
        r_re, r_im = rel[:, :half], rel[:, half:]
        d_head = jnp.concatenate([q_re * r_re + q_im * r_im, q_im * r_re - q_re * r_im], axis=1)
        term = tn(picks[r], d_head.astype(BF))
        own = term if own is None else own + term
    grads[2 * rows : 3 * rows] = own.astype(BF)
    wide = lax.broadcasted_iota(jnp.int32, (edges, 128), 1)
    both = jnp.where(wide == 0, losses[0], jnp.where(wide == 1, losses[1], 0.0))
    loss_out[...] = jnp.transpose(both)[0:2]

    dpre[...] = (nt(grads[...], w2[...]) * slope[...]).astype(BF)
    rows_1, rows_2 = g1_out.shape[0], g2_out.shape[0]
    part_1, part_w2 = rows_1 // na, rows_2 // na
    block = part_1 + part_w2
    width = w2.shape[1] // na
    halves = ng // 2

    def slice_of(which, put):
        first_1 = pl.multiple_of(which * rows_1, rows_1)
        first_2 = pl.multiple_of(which * rows_2, rows_2)
        t1 = mm(xt[pl.ds(first_1, rows_1), 0 : 3 * rows], dpre[...])
        t2 = mm(ht[pl.ds(first_2, rows_2), 0 : 3 * rows], grads[...])
        for i in range(na):
            put(i, t2[i * part_w2 : (i + 1) * part_w2], t1[i * part_1 : (i + 1) * part_1])

    for gh in range(halves):

        def put_send(i, low, high, gh=gh):
            core_send[gh, i, 0:part_w2] = low.astype(BF)
            core_send[gh, i, part_w2:block] = high.astype(BF)

        slice_of(2 * gh + 1 - c, put_send)
        push(core_send.at[gh], core_recv.at[gh], sem_core.at[gh], other_core)
    for gh in range(halves):

        def put_own(i, low, high, gh=gh):
            total[gh, i, 0:part_w2] = low
            total[gh, i, part_w2:block] = high

        slice_of(2 * gh + c, put_own)

    a = c * x + (1 - c) * y
    b = c * y + (1 - c) * x

    def along_a(k):
        return dev(zh, c * k + (1 - c) * x, c * y + (1 - c) * k, c, g)

    def along_b(k):
        return dev(zh, c * x + (1 - c) * k, c * k + (1 - c) * y, c, g)

    for gh in range(halves):
        arrived(core_recv.at[gh], sem_core.at[gh])
        total[gh] = total[gh] + core_recv[gh].astype(F32)
        send_1[gh] = total[gh].astype(BF)
        for j in range(1, na):
            k = rem(a + j, na)
            push(send_1.at[gh, k], recv_1.at[a, gh], sem_1.at[a, gh], along_a(k))
    for gh in range(halves):
        part = total[gh, a]
        for j in range(1, na):
            k = rem(a + j, na)
            arrived(recv_1.at[k, gh], sem_1.at[k, gh])
            part = part + recv_1[k, gh].astype(F32)
        for i in range(na):
            part_2[i, gh] = part[:, i * width : (i + 1) * width]
            send_2[i, gh] = part[:, i * width : (i + 1) * width].astype(BF)
    for j in range(1, na):
        k = rem(b + j, na)
        push(send_2.at[k], recv_2.at[b], sem_2.at[b], along_b(k))
    part = part_2[b]
    for j in range(1, na):
        k = rem(b + j, na)
        arrived(recv_2.at[k], sem_2.at[k])
        part = part + recv_2[k].astype(F32)
    send_z[...] = part.astype(BF)

    matched = rem(g + c, 2) == 0
    conditional = []
    for gh in range(halves):
        for zp in range(nzh):
            to = 2 * gh + c
            elsewhere = jnp.logical_or(rem(zh + zp, nzh) != zh, to != g)
            conditional.append((elsewhere, gh, zp, counter[0]))

            @pl.when(elsewhere)
            def _(gh=gh, zp=zp, to=to):
                push(
                    send_z.at[gh],
                    recv_z.at[z],
                    sem_rz.at[z],
                    dev(rem(zh + zp, nzh), x, y, c, to),
                    keep=False,
                )

    base_s = counter[0]

    @pl.when(matched)
    def _():
        recv_z[z] = send_z[div(g, 2)]
        for k in range(1, nz):
            source = rem(z + k, nz)
            arrived(recv_z.at[source], sem_rz.at[source])
        piece = jnp.zeros((block, width), F32)
        for k in range(nz):
            piece = piece + recv_z[k].astype(F32)
        gathered[a, b, 0:block] = piece
        gathered[a, b, block : block + 8] = jnp.full((8, width), jnp.sum(piece * piece), F32)
        mine = []
        for j in range(1, na):
            mine.append(
                push(
                    gathered.at[a, b],
                    gathered.at[a, b],
                    sem_b.at[b],
                    along_b(rem(b + j, na)),
                    keep=False,
                )
            )
        for j in range(1, na):
            k = rem(b + j, na)
            arrived(gathered.at[a, k], sem_b.at[k])
        for j in range(1, na):
            mine.append(
                push(
                    gathered.at[a],
                    gathered.at[a],
                    sem_a.at[a],
                    along_a(rem(a + j, na)),
                    keep=False,
                )
            )
        mine.append(push(gathered.at[a], gathered.at[a], sem_g.at[a], other_core, keep=False))
        for j in range(1, na):
            k = rem(a + j, na)
            arrived(gathered.at[k], sem_a.at[k])
            mine.append(push(gathered.at[k], gathered.at[k], sem_g.at[k], other_core, keep=False))
        ss = jnp.zeros((8, width), F32)
        for i in range(na):
            for k in range(na):
                ss = ss + gathered[i, k, block : block + 8]
        squares[g] = ss
        for k in range(1, ng):
            for cc in range(2):
                mine.append(
                    push(
                        squares.at[g],
                        squares.at[g],
                        sem_s.at[g],
                        dev(zh, x, y, cc, rem(g + k, ng)),
                        keep=False,
                    )
                )
        mine.append(push(squares.at[g], squares.at[g], sem_s.at[g], other_core, keep=False))
        for copy in mine:
            copy.wait_send()

    @pl.when(jnp.logical_not(matched))
    def _():
        arrived(squares.at[g], sem_s.at[g])
        for k in range(na):
            arrived(gathered.at[k], sem_g.at[k])

    for k in range(1, ng):
        source = rem(g + k, ng)
        arrived(squares.at[source], sem_s.at[source])
    ss = squares[0]
    for k in range(1, ng):
        ss = ss + squares[k]
    count = float(ng * block * na * na * width)
    factor = jnp.minimum(1.0, math.sqrt(count) / jnp.sqrt(ss + 1e-06))[0:1]
    for i in range(na):
        for k in range(na):
            g2_out[i * part_w2 : (i + 1) * part_w2, k * width : (k + 1) * width] = (
                gathered[i, k, 0:part_w2] * factor
            )
            g1_out[i * part_1 : (i + 1) * part_1, k * width : (k + 1) * width] = (
                gathered[i, k, part_w2:block] * factor
            )

    for copy in pending:
        copy.wait_send()
    for elsewhere, gh, zp, index in conditional:

        @pl.when(elsewhere)
        def _(gh=gh, zp=zp, index=index):
            pltpu.make_async_remote_copy(
                src_ref=send_z.at[gh],
                dst_ref=recv_z.at[z],
                send_sem=send_sem.at[index],
                recv_sem=sem_rz.at[z],
                device_id=dev(rem(zh + zp, nzh), x, y, c, 2 * gh + c),
                device_id_type=MESH,
            ).wait_send()


def per_device(dims, features, w_first, w_second, table, heads, relations, tails, negatives, partner):
    nzh, na, ng = dims
    nz = nzh * ng
    own, d_in = features.shape
    d_hid, d_enc = w_second.shape
    edges = heads.shape[1]
    rows = own * ng
    rows_1, rows_2 = d_in // ng, d_hid // ng
    block, width, halves = (rows_1 + rows_2) // na, d_enc // na, ng // 2
    lanes = max(256, 3 * rows)
    vmem = pl.BlockSpec(memory_space=pltpu.VMEM)
    anyspace = pl.BlockSpec(memory_space=pl.ANY)
    smem = pl.BlockSpec(memory_space=pltpu.SMEM)
    V, S = pltpu.VMEM, pltpu.SemaphoreType.DMA
    return pl.pallas_call(
        functools.partial(body, dims),
        out_shape=(
            jax.ShapeDtypeStruct(heads.shape, F32),
            jax.ShapeDtypeStruct((rows_1, d_hid), F32),
            jax.ShapeDtypeStruct((rows_2, d_enc), F32),
        ),
        in_specs=[vmem, anyspace, anyspace, anyspace, vmem, vmem, vmem, vmem, smem],
        out_specs=(vmem, vmem, vmem),
        scratch_shapes=[
            V(w_first.shape, BF),
            V(w_second.shape, BF),
            V(table.shape, BF),
            V((8, edges), F32),
            V((2 * na, own, d_in), BF),
            V((2, own, d_in), BF),
            V((na, 2, own, d_in), BF),
            V((nz, 2, own, d_in), BF),
            V((ng, own, d_in), BF),
            V((2, edges, d_enc), BF),
            V((2, edges, d_enc), BF),
            V((3 * rows, d_enc), BF),
            V((3 * rows, d_hid), F32),
            V((3 * rows, d_enc), BF),
            V((3 * rows, d_hid), BF),
            V((d_in, lanes), BF),
            V((d_hid, lanes), BF),
            V((halves, na, block, d_enc), BF),
            V((halves, na, block, d_enc), BF),
            V((halves, na, block, d_enc), F32),
            V((halves, na, block, d_enc), BF),
            V((na, halves, block, d_enc), BF),
            V((na, halves, block, width), F32),
            V((na, halves, block, width), BF),
            V((na, halves, block, width), BF),
            V((halves, block, width), BF),
            V((nz, block, width), BF),
            V((na, na, block + 8, width), F32),
            V((ng, 8, width), F32),
            S((3,)),
            S((128,)),
            S((2 * na,)),
            S((na,)),
            S((nz,)),
            S((ng,)),
            S((halves,)),
            S((na, halves)),
            S((na,)),
            S((nz,)),
            S((na,)),
            S((na,)),
            S((na,)),
            S((ng,)),
        ],
        compiler_params=pltpu.CompilerParams(
            collective_id=0, has_side_effects=True, vmem_limit_bytes=56 * 1024 * 1024
        ),
        name="step",
    )(features, w_first, w_second, table, heads, relations, tails, negatives, partner)


def solution(mesh):
    ng = mesh.shape["grp"]
    na = math.isqrt(mesh.shape["dom"] // 4)
    return jax.shard_map(
        functools.partial(per_device, (2, na, ng)),
        mesh=mesh,
        in_specs=(
            P(("dom", "grp"), None),
            P(),
            P(),
            P(),
            P(None, ("dom", "grp")),
            P(None, ("dom", "grp")),
            P(None, ("dom", "grp")),
            P(),
            P(),
        ),
        out_specs=(P(None, ("dom", "grp")), P("grp", None), P("grp", None)),
        check_vma=False,
    )
```

```python
import functools
import math

import jax
import jax.numpy as jnp
from jax import lax
from jax.experimental import pallas as pl
from jax.experimental.pallas import tpu as pltpu
from jax.sharding import PartitionSpec as P

MESH = pl.DeviceIdType.MESH
BF = jnp.bfloat16
F32 = jnp.float32
HOP = 3


def mm(a, b):
    return jnp.dot(a, b, preferred_element_type=F32)


def nt(a, b):
    return lax.dot_general(a, b, (((1,), (1,)), ((), ())), preferred_element_type=F32)


def tn(a, b):
    return lax.dot_general(a, b, (((0,), (0,)), ((), ())), preferred_element_type=F32)


def sigmoid(v):
    return 1.0 / (1.0 + jnp.exp(-v))


def softplus(v):
    return jnp.maximum(v, 0.0) + jnp.log1p(jnp.exp(-jnp.abs(v)))


def body(
    dims,
    feat_hbm,
    w1_hbm,
    w2_hbm,
    table_hbm,
    heads_hbm,
    rels_hbm,
    tails_hbm,
    negs_hbm,
    partner_hbm,
    loss_out,
    gathered,
    norm_out,
    feat,
    w1,
    w2,
    table,
    heads,
    rels,
    tails,
    negs,
    partner,
    ids,
    buf_y,
    send_x,
    buf_x,
    buf_z,
    buf_o,
    rel_rows,
    query,
    enc,
    slope,
    grads,
    dpre,
    xt,
    ht,
    core_send,
    core_recv,
    total,
    send_1,
    recv_1,
    part_2,
    send_2,
    recv_2,
    send_z,
    recv_z,
    parts_sq,
    squares,
    load_sem,
    send_sem,
    sem_y,
    sem_x,
    sem_z,
    sem_o,
    sem_core,
    sem_1,
    sem_2,
    sem_rz,
    sem_q,
    sem_p,
    sem_c,
    sem_s,
):
    nzh, na, ng = dims
    nz = nzh * ng
    rem, div = lax.rem, lax.div
    dom = lax.axis_index("dom")
    g = lax.axis_index("grp")
    c = rem(dom, 2)
    y = rem(div(dom, 2), na)
    x = rem(div(dom, 2 * na), na)
    zh = div(dom, 2 * na * na)
    z = zh * ng + g
    bits = na.bit_length() - 1

    def dev(zh_, x_, y_, c_, g_):
        return (((zh_ * na + x_) * na + y_) * 2 + c_, g_)

    def xor(v, k):
        out = 0
        for b in range(bits):
            out = out + rem(div(v, 1 << b) + (k >> b & 1), 2) * (1 << b)
        return out

    def on_ring(step):
        to = rem(z + step + nz, nz)
        return dev(div(to, ng), x, y, c, rem(to, ng))

    other_core = dev(zh, x, y, 1 - c, g)
    pending = []
    counter = [0]

    def push(src, dst, sem, target, keep=True):
        copy = pltpu.make_async_remote_copy(
            src_ref=src,
            dst_ref=dst,
            send_sem=send_sem.at[counter[0]],
            recv_sem=sem,
            device_id=target,
            device_id_type=MESH,
        )
        counter[0] += 1
        copy.start()
        if keep:
            pending.append(copy)
        return copy

    def arrived(dst, sem):
        pltpu.make_async_remote_copy(
            src_ref=dst,
            dst_ref=dst,
            send_sem=send_sem.at[0],
            recv_sem=sem,
            device_id=other_core,
            device_id_type=MESH,
        ).wait_recv()

    def ring(buf, sem):
        reach = {1: nz // 2, -1: nz - 1 - nz // 2}
        seen = set()
        for base in range(0, reach[1], HOP):
            for way in (1, -1):
                if base >= reach[way]:
                    continue
                source = rem(z - way * base + nz, nz)
                if base:
                    arrived(buf.at[source], sem.at[source])
                    seen.add(-way * base)
                for step in range(min(HOP, reach[way] - base), 0, -1):
                    push(buf.at[source], buf.at[source], sem.at[source], on_ring(way * step))
            yield
        for way in (1, -1):
            for dist in range(1, reach[way] + 1):
                if -way * dist not in seen:
                    source = rem(z - way * dist + nz, nz)
                    arrived(buf.at[source], sem.at[source])

    barrier = pltpu.get_barrier_semaphore()
    peers = [
        dev(zh, x, xor(y, k >> 1), rem(c + (k & 1), 2), g) for k in range(1, 2 * na)
    ]
    peers += [dev(zh, xor(x, k), y, c, g) for k in range(1, na)]
    near = min(HOP, nz // 2)
    peers += [on_ring(k) for k in range(1, nz) if min(k, nz - k) <= near]
    for peer in peers:
        pl.semaphore_signal(barrier, inc=1, device_id=peer, device_id_type=MESH)

    pairs = (
        (feat_hbm, feat),
        (feat_hbm, buf_y.at[0]),
        (feat_hbm, buf_o.at[z]),
        (partner_hbm, partner),
        (heads_hbm, heads),
        (rels_hbm, rels),
        (tails_hbm, tails),
        (negs_hbm, negs),
        (table_hbm, table),
        (w1_hbm, w1),
        (w2_hbm, w2),
    )
    loads = []
    for i, (src, dst) in enumerate(pairs):
        loads.append(pltpu.make_async_copy(src, dst, load_sem.at[i]))
        loads[-1].start()
    for load in loads[0:3]:
        load.wait()
    pl.semaphore_wait(barrier, len(peers))

    for k in range(1, 2 * na):
        push(feat, buf_y.at[k], sem_y.at[k], dev(zh, x, xor(y, k >> 1), rem(c + (k & 1), 2), g))
    own_ring = ring(buf_o, sem_o)
    next(own_ring)

    for load in loads[3:9]:
        load.wait()
    ids[0:2] = heads[...].astype(F32)
    ids[2:4] = rels[...].astype(F32)
    ids[4:6] = tails[...].astype(F32)
    ids[6:8] = jnp.zeros_like(ids[6:8])
    columns = jnp.transpose(ids[...])
    nrel = table.shape[0]
    edges = heads.shape[1]
    for r in range(2):
        pick = lax.broadcasted_iota(jnp.int32, (edges, nrel), 1).astype(F32) == columns[:, 2 + r : 3 + r]
        rel_rows[r] = mm(pick.astype(BF), table[...]).astype(BF)

    masks = [partner[r, 0] for r in range(2)]
    for k in range(1, 2 * na):
        arrived(buf_y.at[k], sem_y.at[k])
    for r in range(2):
        send_x[r] = buf_y[masks[r] % (2 * na)]
    for k in range(1, na):
        push(send_x, buf_x.at[k], sem_x.at[k], dev(zh, xor(x, k), y, c, g))
    next(own_ring, None)
    buf_x[0] = send_x[...]
    for k in range(1, na):
        arrived(buf_x.at[k], sem_x.at[k])
    for r in range(2):
        buf_z[z, r] = buf_x[(masks[r] // (2 * na)) % na, r]

    far_ring = ring(buf_z, sem_z)
    next(far_ring)
    for _ in own_ring:
        pass

    for load in loads[9:]:
        load.wait()
    rows = 8 * ng
    half = w2.shape[1] // 2
    lane = lax.broadcasted_iota(jnp.int32, (edges, rows), 1).astype(F32)

    def encode(x_rows, first, count, at):
        pre = mm(x_rows, w1[...])
        s = sigmoid(pre)
        hidden = (pre * s).astype(BF)
        enc[first : first + count] = mm(hidden, w2[...]).astype(BF)
        slope[first : first + count] = s * (1.0 + pre * (1.0 - s))
        xt[:, at : at + count] = jnp.transpose(x_rows)
        ht[:, at : at + count] = jnp.transpose(hidden)

    own_x = buf_o[pl.ds(zh * ng, ng)].astype(F32).reshape(rows, feat.shape[1]).astype(BF)
    encode(own_x, 2 * rows, rows, 2 * rows)
    picks = []
    for r in range(2):
        head_pick = (lane == columns[:, r : r + 1]).astype(BF)
        picks.append(head_pick)
        head = mm(head_pick, enc[2 * rows : 3 * rows])
        rel = rel_rows[r].astype(F32)
        h_re, h_im = head[:, :half], head[:, half:]
        r_re, r_im = rel[:, :half], rel[:, half:]
        query[r, :, :half] = (h_re * r_re - h_im * r_im).astype(BF)
        query[r, :, half:] = (h_re * r_im + h_im * r_re).astype(BF)
    counts = []
    nneg = negs.shape[1]
    for r in range(2):
        hit = lax.broadcasted_iota(jnp.int32, (rows, nneg), 0) == negs[r : r + 1, :]
        counts.append(nt(jnp.ones((8, nneg), BF), hit.astype(F32).astype(BF))[0:1])
    for _ in far_ring:
        pass

    far = []
    for r in range(2):
        half_of = rem(zh + (masks[r] // (2 * na * na)) % 2, 2)
        rows_r = buf_z[pl.ds(half_of * ng, ng), r]
        far.append(rows_r.astype(F32).reshape(rows, feat.shape[1]))
    encode(jnp.concatenate(far, axis=0).astype(BF), 0, 2 * rows, 0)

    own = None
    losses = []
    for r in range(2):
        other = enc[r * rows : (r + 1) * rows]
        q = query[r]
        score = nt(q, other)
        tail_pick = jnp.where(lane == columns[:, 4 + r : 5 + r], 1.0, 0.0)
        positive = jnp.sum(score * tail_pick, axis=1, keepdims=True)
        losses.append(
            softplus(-positive) + jnp.sum(softplus(score) * counts[r], axis=1, keepdims=True) / nneg
        )
        weight_neg = (sigmoid(score) / nneg).astype(BF).astype(F32)
        weight_pos = -sigmoid(-positive)
        weight = (weight_neg * counts[r] + tail_pick * weight_pos).astype(BF)
        d_query = mm(weight, other)
        grads[r * rows : (r + 1) * rows] = tn(weight, q).astype(BF)
        rel = rel_rows[r].astype(F32)
        q_re, q_im = d_query[:, :half], d_query[:, half:]
        r_re, r_im = rel[:, :half], rel[:, half:]
        d_head = jnp.concatenate([q_re * r_re + q_im * r_im, q_im * r_re - q_re * r_im], axis=1)
        term = tn(picks[r], d_head.astype(BF))
        own = term if own is None else own + term
    grads[2 * rows : 3 * rows] = own.astype(BF)
    wide = lax.broadcasted_iota(jnp.int32, (edges, 128), 1)
    both = jnp.where(wide == 0, losses[0], jnp.where(wide == 1, losses[1], 0.0))
    loss_out[...] = jnp.transpose(both)[0:2]

    dpre[...] = (nt(grads[...], w2[...]) * slope[...]).astype(BF)
    rows_1, rows_2 = w1.shape[0] // ng, w2.shape[0] // ng
    part_1, part_w2 = rows_1 // na, rows_2 // na
    block = part_1 + part_w2
    width = w2.shape[1] // na
    halves = ng // 2

    def slice_of(which, put):
        first_1 = pl.multiple_of(which * rows_1, rows_1)
        first_2 = pl.multiple_of(which * rows_2, rows_2)
        t1 = mm(xt[pl.ds(first_1, rows_1), 0 : 3 * rows], dpre[...])
        t2 = mm(ht[pl.ds(first_2, rows_2), 0 : 3 * rows], grads[...])
        for i in range(na):
            put(i, t2[i * part_w2 : (i + 1) * part_w2], t1[i * part_1 : (i + 1) * part_1])

    for gh in range(halves):

        def put_send(i, low, high, gh=gh):
            core_send[gh, i, 0:part_w2] = low.astype(BF)
            core_send[gh, i, part_w2:block] = high.astype(BF)

        slice_of(2 * gh + 1 - c, put_send)
        push(core_send.at[gh], core_recv.at[gh], sem_core.at[gh], other_core)
    for gh in range(halves):

        def put_own(i, low, high, gh=gh):
            total[gh, i, 0:part_w2] = low
            total[gh, i, part_w2:block] = high

        slice_of(2 * gh + c, put_own)

    a = c * x + (1 - c) * y
    b = c * y + (1 - c) * x

    def along_a(k):
        return dev(zh, c * k + (1 - c) * x, c * y + (1 - c) * k, c, g)

    def in_plane(k):
        ka, kb = div(k, na), rem(k, na)
        return dev(zh, c * ka + (1 - c) * kb, c * kb + (1 - c) * ka, c, g)

    def along_b(k):
        return dev(zh, c * x + (1 - c) * k, c * k + (1 - c) * y, c, g)

    for gh in range(halves):
        arrived(core_recv.at[gh], sem_core.at[gh])
        total[gh] = total[gh] + core_recv[gh].astype(F32)
        send_1[gh] = total[gh].astype(BF)
        for j in range(1, na):
            k = rem(a + j, na)
            push(send_1.at[gh, k], recv_1.at[a, gh], sem_1.at[a, gh], along_a(k))
    for gh in range(halves):
        part = total[gh, a]
        for j in range(1, na):
            k = rem(a + j, na)
            arrived(recv_1.at[k, gh], sem_1.at[k, gh])
            part = part + recv_1[k, gh].astype(F32)
        for i in range(na):
            part_2[i, gh] = part[:, i * width : (i + 1) * width]
            send_2[i, gh] = part[:, i * width : (i + 1) * width].astype(BF)
    for j in range(1, na):
        k = rem(b + j, na)
        push(send_2.at[k], recv_2.at[b], sem_2.at[b], along_b(k))
    part = part_2[b]
    for j in range(1, na):
        k = rem(b + j, na)
        arrived(recv_2.at[k], sem_2.at[k])
        part = part + recv_2[k].astype(F32)
    send_z[...] = part.astype(BF)

    matched = rem(g + c, 2) == 0
    conditional = []
    for gh in range(halves):
        for zp in range(nzh):
            to = 2 * gh + c
            elsewhere = jnp.logical_or(rem(zh + zp, nzh) != zh, to != g)
            conditional.append((elsewhere, gh, zp, counter[0]))

            @pl.when(elsewhere)
            def _(gh=gh, zp=zp, to=to):
                push(
                    send_z.at[gh],
                    recv_z.at[z],
                    sem_rz.at[z],
                    dev(rem(zh + zp, nzh), x, y, c, to),
                    keep=False,
                )

    @pl.when(matched)
    def _():
        recv_z[z] = send_z[div(g, 2)]
        for k in range(1, nz):
            source = rem(z + k, nz)
            arrived(recv_z.at[source], sem_rz.at[source])
        piece = jnp.zeros((block, width), F32)
        for k in range(nz):
            piece = piece + recv_z[k].astype(F32)
        slot = a * na + b
        places = na * na
        parts_sq[slot] = jnp.full((1, width), jnp.sum(piece * piece), F32)
        mine = []
        for t in range(1, places):
            to = rem(slot + t, places)
            mine.append(
                push(parts_sq.at[slot], parts_sq.at[slot], sem_q.at[slot], in_plane(to), keep=False)
            )
        gathered[slot] = piece
        for t in range(1, places):
            to = rem(slot + t, places)
            mine.append(
                push(gathered.at[slot], gathered.at[slot], sem_p.at[slot], in_plane(to), keep=False)
            )
        mine.append(push(gathered.at[slot], gathered.at[slot], sem_c.at[slot], other_core, keep=False))
        for t in range(1, places):
            source = rem(slot + t, places)
            arrived(parts_sq.at[source], sem_q.at[source])
        ss = parts_sq[0]
        for i in range(1, places):
            ss = ss + parts_sq[i]
        squares[g] = ss
        for k in range(ng - 1, 0, -1):
            for cc in range(2):
                mine.append(
                    push(
                        squares.at[g],
                        squares.at[g],
                        sem_s.at[g],
                        dev(zh, x, y, cc, rem(g + k, ng)),
                        keep=False,
                    )
                )
        mine.append(push(squares.at[g], squares.at[g], sem_s.at[g], other_core, keep=False))
        for t in range(places - 1, 0, -1):
            source = rem(slot + t, places)
            arrived(gathered.at[source], sem_p.at[source])
            mine.append(
                push(gathered.at[source], gathered.at[source], sem_c.at[source], other_core, keep=False)
            )
        for copy in mine:
            copy.wait_send()

    @pl.when(jnp.logical_not(matched))
    def _():
        arrived(squares.at[g], sem_s.at[g])
        for k in range(na * na):
            arrived(gathered.at[k], sem_c.at[k])

    for k in range(1, ng):
        source = rem(g + k, ng)
        arrived(squares.at[source], sem_s.at[source])
    ss = squares[0]
    for k in range(1, ng):
        ss = ss + squares[k]
    norm_out[...] = ss

    for copy in pending:
        copy.wait_send()
    for elsewhere, gh, zp, index in conditional:

        @pl.when(elsewhere)
        def _(gh=gh, zp=zp, index=index):
            pltpu.make_async_remote_copy(
                src_ref=send_z.at[gh],
                dst_ref=recv_z.at[z],
                send_sem=send_sem.at[index],
                recv_sem=sem_rz.at[z],
                device_id=dev(rem(zh + zp, nzh), x, y, c, 2 * gh + c),
                device_id_type=MESH,
            ).wait_send()


def finish(na, count, loss_in, pieces, squares, loss_out, g1_out, g2_out):
    low = g2_out.shape[0] // na
    high = g1_out.shape[0] // na
    width = pieces.shape[2]
    factor = jnp.minimum(1.0, math.sqrt(count) / jnp.sqrt(squares[...] + 1e-06))
    loss_out[...] = loss_in[...]
    for i in range(na):
        for k in range(na):
            column = slice(k * width, (k + 1) * width)
            g2_out[i * low : (i + 1) * low, column] = pieces[i * na + k, 0:low] * factor
            g1_out[i * high : (i + 1) * high, column] = pieces[i * na + k, low:] * factor


def per_device(dims, features, w_first, w_second, table, heads, relations, tails, negatives, partner):
    nzh, na, ng = dims
    nz = nzh * ng
    own, d_in = features.shape
    d_hid, d_enc = w_second.shape
    edges = heads.shape[1]
    rows = own * ng
    rows_1, rows_2 = d_in // ng, d_hid // ng
    block, width, halves = (rows_1 + rows_2) // na, d_enc // na, ng // 2
    lanes = max(256, 3 * rows)
    vmem = pl.BlockSpec(memory_space=pltpu.VMEM)
    hbm = pl.BlockSpec(memory_space=pltpu.HBM)
    V, S = pltpu.VMEM, pltpu.SemaphoreType.DMA
    loss, pieces, squares = pl.pallas_call(
        functools.partial(body, dims),
        out_shape=(
            jax.ShapeDtypeStruct(heads.shape, F32),
            jax.ShapeDtypeStruct((na * na, block, width), F32),
            jax.ShapeDtypeStruct((1, width), F32),
        ),
        in_specs=[hbm] * 9,
        out_specs=(vmem, vmem, vmem),
        scratch_shapes=[
            V(features.shape, BF),
            V(w_first.shape, BF),
            V(w_second.shape, BF),
            V(table.shape, BF),
            V(heads.shape, jnp.int32),
            V(relations.shape, jnp.int32),
            V(tails.shape, jnp.int32),
            V(negatives.shape, jnp.int32),
            pltpu.SMEM(partner.shape, jnp.int32),
            V((8, edges), F32),
            V((2 * na, own, d_in), BF),
            V((2, own, d_in), BF),
            V((na, 2, own, d_in), BF),
            V((nz, 2, own, d_in), BF),
            V((nz, own, d_in), BF),
            V((2, edges, d_enc), BF),
            V((2, edges, d_enc), BF),
            V((3 * rows, d_enc), BF),
            V((3 * rows, d_hid), F32),
            V((3 * rows, d_enc), BF),
            V((3 * rows, d_hid), BF),
            V((d_in, lanes), BF),
            V((d_hid, lanes), BF),
            V((halves, na, block, d_enc), BF),
            V((halves, na, block, d_enc), BF),
            V((halves, na, block, d_enc), F32),
            V((halves, na, block, d_enc), BF),
            V((na, halves, block, d_enc), BF),
            V((na, halves, block, width), F32),
            V((na, halves, block, width), BF),
            V((na, halves, block, width), BF),
            V((halves, block, width), BF),
            V((nz, block, width), BF),
            V((na * na, 1, width), F32),
            V((ng, 1, width), F32),
            S((11,)),
            S((160,)),
            S((2 * na,)),
            S((na,)),
            S((nz,)),
            S((nz,)),
            S((halves,)),
            S((na, halves)),
            S((na,)),
            S((nz,)),
            S((na * na,)),
            S((na * na,)),
            S((na * na,)),
            S((ng,)),
        ],
        compiler_params=pltpu.CompilerParams(
            collective_id=0, has_side_effects=True, vmem_limit_bytes=24 * 1024 * 1024
        ),
        name="step",
    )(features, w_first, w_second, table, heads, relations, tails, negatives, partner)
    return pl.pallas_call(
        functools.partial(finish, na, float(w_first.size + w_second.size)),
        out_shape=(
            jax.ShapeDtypeStruct(heads.shape, F32),
            jax.ShapeDtypeStruct((rows_1, d_hid), F32),
            jax.ShapeDtypeStruct((rows_2, d_enc), F32),
        ),
        in_specs=[vmem] * 3,
        out_specs=(vmem, vmem, vmem),
        name="finish",
    )(loss, pieces, squares)


def solution(mesh):
    ng = mesh.shape["grp"]
    na = math.isqrt(mesh.shape["dom"] // 4)
    return jax.shard_map(
        functools.partial(per_device, (2, na, ng)),
        mesh=mesh,
        in_specs=(
            P(("dom", "grp"), None),
            P(),
            P(),
            P(),
            P(None, ("dom", "grp")),
            P(None, ("dom", "grp")),
            P(None, ("dom", "grp")),
            P(),
            P(),
        ),
        out_specs=(P(None, ("dom", "grp")), P("grp", None), P("grp", None)),
        check_vma=False,
    )
```

```python
import functools
import math

import jax
import jax.numpy as jnp
from jax import lax
from jax.experimental import pallas as pl
from jax.experimental.pallas import tpu as pltpu
from jax.sharding import PartitionSpec as P

MESH = pl.DeviceIdType.MESH
BF = jnp.bfloat16
F32 = jnp.float32
HOP = 3
NEAR = 4
RELAY = {0: (4, 2, 1), 2: (1,), 4: (4, 2, 1), 6: (1,)}


def mm(a, b):
    return jnp.dot(a, b, preferred_element_type=F32)


def nt(a, b):
    return lax.dot_general(a, b, (((1,), (1,)), ((), ())), preferred_element_type=F32)


def tn(a, b):
    return lax.dot_general(a, b, (((0,), (0,)), ((), ())), preferred_element_type=F32)


def sigmoid(v):
    return 1.0 / (1.0 + jnp.exp(-v))


def softplus(v):
    return jnp.maximum(v, 0.0) + jnp.log1p(jnp.exp(-jnp.abs(v)))


def body(
    dims,
    feat_hbm,
    w1_hbm,
    w2_hbm,
    table_hbm,
    heads_hbm,
    rels_hbm,
    tails_hbm,
    negs_hbm,
    partner_hbm,
    loss_out,
    gathered,
    norm_out,
    feat,
    w1,
    w2,
    table,
    heads,
    rels,
    tails,
    negs,
    partner,
    ids,
    buf_y,
    send_x,
    buf_x,
    buf_z,
    buf_o,
    rel_rows,
    query,
    enc,
    slope,
    grads,
    dpre,
    xt,
    ht,
    core_send,
    core_recv,
    total,
    send_1,
    recv_1,
    part_2,
    send_2,
    recv_2,
    send_z,
    recv_z,
    parts_sq,
    squares,
    load_sem,
    send_sem,
    line_sem,
    sem_y,
    sem_x,
    sem_z,
    sem_o,
    sem_core,
    sem_1,
    sem_2,
    sem_rz,
    sem_q,
    sem_p,
    sem_c,
    sem_s,
    sem_t,
):
    nzh, na, ng = dims
    nz = nzh * ng
    rem, div = lax.rem, lax.div
    dom = lax.axis_index("dom")
    g = lax.axis_index("grp")
    c = rem(dom, 2)
    y = rem(div(dom, 2), na)
    x = rem(div(dom, 2 * na), na)
    zh = div(dom, 2 * na * na)
    z = zh * ng + g
    bits = na.bit_length() - 1

    def dev(zh_, x_, y_, c_, g_):
        return (((zh_ * na + x_) * na + y_) * 2 + c_, g_)

    def xor(v, k):
        out = 0
        for b in range(bits):
            out = out + rem(div(v, 1 << b) + (k >> b & 1), 2) * (1 << b)
        return out

    def on_ring(step):
        to = rem(z + step + nz, nz)
        return dev(div(to, ng), x, y, c, rem(to, ng))

    other_core = dev(zh, x, y, 1 - c, g)
    conditional = []
    sent = {}

    def push(src, dst, sem, target, group):
        sent[group] = sent.get(group, 0) + 1
        pltpu.make_async_remote_copy(
            src_ref=src,
            dst_ref=dst,
            send_sem=send_sem.at[group],
            recv_sem=sem,
            device_id=target,
            device_id_type=MESH,
        ).start()

    def all_sent(group, like):
        pltpu.make_async_remote_copy(
            src_ref=like,
            dst_ref=like,
            send_sem=send_sem.at[group],
            recv_sem=sem_core.at[0],
            device_id=other_core,
            device_id_type=MESH,
        ).wait_send()

    def arrived(dst, sem):
        pltpu.make_async_remote_copy(
            src_ref=dst,
            dst_ref=dst,
            send_sem=send_sem.at[0],
            recv_sem=sem,
            device_id=other_core,
            device_id_type=MESH,
        ).wait_recv()

    def ring(buf, sem, group):
        pieces = [(r, way) for r in range(2) for way in ((1, -1) if r == 0 else (-1, 1))]

        def last(r, way):
            return nz // 2 if (way == 1) == (r == 0) else nz // 2 - 1

        waited = set()
        for base in sorted(RELAY):
            for r, way in pieces:
                if base > last(r, way):
                    continue
                source = rem(z - way * base + nz, nz)
                held, flag = buf.at[source, r], sem.at[source, r]
                if base:
                    arrived(held, flag)
                    waited.add((r, way, base))
                for step in RELAY[base]:
                    if base + step <= last(r, way):
                        push(held, held, flag, on_ring(way * step), group)
            yield
        for r, way in pieces:
            for dist in range(1, last(r, way) + 1):
                if (r, way, dist) not in waited:
                    source = rem(z - way * dist + nz, nz)
                    arrived(buf.at[source, r], sem.at[source, r])

    def push_if(cond, *what):
        index = len(conditional)

        def make():
            src, dst, sem, target = what
            return pltpu.make_async_remote_copy(
                src_ref=src,
                dst_ref=dst,
                send_sem=line_sem.at[index],
                recv_sem=sem,
                device_id=target,
                device_id_type=MESH,
            )

        @pl.when(cond)
        def _():
            make().start()

        conditional.append((cond, make))

    def arrived_if(cond, *what):
        @pl.when(cond)
        def _():
            arrived(*what)

    def line(buf, sem):
        def within(k):
            return jnp.logical_and(k >= 0, k < ng)

        seen = set()
        for base in range(0, ng - 1, HOP):
            for way in (1, -1):
                source = g - way * base
                there = within(source)
                held = buf.at[rem(source + ng, ng)]
                flag = sem.at[rem(source + ng, ng)]
                if base:
                    arrived_if(there, held, flag)
                    seen.add(-way * base)
                for step in range(min(HOP, ng - 1 - base), 0, -1):
                    to = g + way * step
                    both = jnp.logical_and(there, within(to))
                    push_if(both, held, held, flag, dev(zh, x, y, c, rem(to + ng, ng)))
            yield
        for way in (1, -1):
            for dist in range(1, ng):
                if -way * dist not in seen:
                    source = rem(g - way * dist + ng, ng)
                    arrived_if(within(g - way * dist), buf.at[source], sem.at[source])

    barrier = pltpu.get_barrier_semaphore()
    peers = [
        dev(zh, x, xor(y, k >> 1), rem(c + (k & 1), 2), g) for k in range(1, 2 * na)
    ]
    peers += [dev(zh, xor(x, k), y, c, g) for k in range(1, na)]
    near = min(NEAR, nz // 2)
    peers += [on_ring(k) for k in range(1, nz) if min(k, nz - k) <= near]
    for peer in peers:
        pl.semaphore_signal(barrier, inc=1, device_id=peer, device_id_type=MESH)

    pairs = (
        (feat_hbm, feat),
        (feat_hbm, buf_y.at[0]),
        (feat_hbm, buf_o.at[g]),
        (partner_hbm, partner),
        (heads_hbm, heads),
        (rels_hbm, rels),
        (tails_hbm, tails),
        (negs_hbm, negs),
        (table_hbm, table),
        (w1_hbm, w1),
        (w2_hbm, w2),
    )
    loads = []
    for i, (src, dst) in enumerate(pairs):
        loads.append(pltpu.make_async_copy(src, dst, load_sem.at[i]))
        loads[-1].start()
    for load in loads[0:3]:
        load.wait()
    pl.semaphore_wait(barrier, len(peers))

    for k in range(1, 2 * na):
        target = dev(zh, x, xor(y, k >> 1), rem(c + (k & 1), 2), g)
        push(feat, buf_y.at[k], sem_y.at[0], target, 0)
    own_ring = line(buf_o, sem_o)
    next(own_ring)

    for load in loads[3:9]:
        load.wait()
    ids[0:2] = heads[...].astype(F32)
    ids[2:4] = rels[...].astype(F32)
    ids[4:6] = tails[...].astype(F32)
    ids[6:8] = jnp.zeros_like(ids[6:8])
    columns = jnp.transpose(ids[...])
    nrel = table.shape[0]
    edges = heads.shape[1]
    for r in range(2):
        pick = lax.broadcasted_iota(jnp.int32, (edges, nrel), 1).astype(F32) == columns[:, 2 + r : 3 + r]
        rel_rows[r] = mm(pick.astype(BF), table[...]).astype(BF)

    masks = [partner[r, 0] for r in range(2)]
    arrived(buf_y.at[pl.ds(1, 2 * na - 1)], sem_y.at[0])
    for r in range(2):
        send_x[r] = buf_y[masks[r] % (2 * na)]
    for k in range(1, na):
        push(send_x, buf_x.at[k], sem_x.at[0], dev(zh, xor(x, k), y, c, g), 1)
    next(own_ring, None)
    buf_x[0] = send_x[...]
    arrived(buf_x.at[pl.ds(1, na - 1)], sem_x.at[0])
    for r in range(2):
        buf_z[z, r] = buf_x[(masks[r] // (2 * na)) % na, r]

    far_ring = ring(buf_z, sem_z, 2)
    next(far_ring)
    for _ in own_ring:
        pass

    for load in loads[9:]:
        load.wait()
    rows = 8 * ng
    half = w2.shape[1] // 2
    lane = lax.broadcasted_iota(jnp.int32, (edges, rows), 1).astype(F32)

    def encode(x_rows, first, count, at):
        pre = mm(x_rows, w1[...])
        s = sigmoid(pre)
        hidden = (pre * s).astype(BF)
        enc[first : first + count] = mm(hidden, w2[...]).astype(BF)
        slope[first : first + count] = s * (1.0 + pre * (1.0 - s))
        xt[:, at : at + count] = jnp.transpose(x_rows)
        ht[:, at : at + count] = jnp.transpose(hidden)

    own_x = buf_o[...].astype(F32).reshape(rows, feat.shape[1]).astype(BF)
    encode(own_x, 2 * rows, rows, 2 * rows)
    picks = []
    for r in range(2):
        head_pick = (lane == columns[:, r : r + 1]).astype(BF)
        picks.append(head_pick)
        head = mm(head_pick, enc[2 * rows : 3 * rows])
        rel = rel_rows[r].astype(F32)
        h_re, h_im = head[:, :half], head[:, half:]
        r_re, r_im = rel[:, :half], rel[:, half:]
        query[r, :, :half] = (h_re * r_re - h_im * r_im).astype(BF)
        query[r, :, half:] = (h_re * r_im + h_im * r_re).astype(BF)
    counts = []
    nneg = negs.shape[1]
    for r in range(2):
        hit = lax.broadcasted_iota(jnp.int32, (rows, nneg), 0) == negs[r : r + 1, :]
        counts.append(nt(jnp.ones((8, nneg), BF), hit.astype(F32).astype(BF))[0:1])
    for _ in far_ring:
        pass

    far = []
    for r in range(2):
        half_of = rem(zh + (masks[r] // (2 * na * na)) % 2, 2)
        rows_r = buf_z[pl.ds(half_of * ng, ng), r]
        far.append(rows_r.astype(F32).reshape(rows, feat.shape[1]))
    encode(jnp.concatenate(far, axis=0).astype(BF), 0, 2 * rows, 0)

    own = None
    losses = []
    for r in range(2):
        other = enc[r * rows : (r + 1) * rows]
        q = query[r]
        score = nt(q, other)
        tail_pick = jnp.where(lane == columns[:, 4 + r : 5 + r], 1.0, 0.0)
        positive = jnp.sum(score * tail_pick, axis=1, keepdims=True)
        losses.append(
            softplus(-positive) + jnp.sum(softplus(score) * counts[r], axis=1, keepdims=True) / nneg
        )
        weight_neg = (sigmoid(score) / nneg).astype(BF).astype(F32)
        weight_pos = -sigmoid(-positive)
        weight = (weight_neg * counts[r] + tail_pick * weight_pos).astype(BF)
        d_query = mm(weight, other)
        grads[r * rows : (r + 1) * rows] = tn(weight, q).astype(BF)
        rel = rel_rows[r].astype(F32)
        q_re, q_im = d_query[:, :half], d_query[:, half:]
        r_re, r_im = rel[:, :half], rel[:, half:]
        d_head = jnp.concatenate([q_re * r_re + q_im * r_im, q_im * r_re - q_re * r_im], axis=1)
        term = tn(picks[r], d_head.astype(BF))
        own = term if own is None else own + term
    grads[2 * rows : 3 * rows] = own.astype(BF)
    wide = lax.broadcasted_iota(jnp.int32, (edges, 128), 1)
    both = jnp.where(wide == 0, losses[0], jnp.where(wide == 1, losses[1], 0.0))
    loss_out[...] = jnp.transpose(both)[0:2]

    dpre[...] = (nt(grads[...], w2[...]) * slope[...]).astype(BF)
    rows_1, rows_2 = w1.shape[0] // ng, w2.shape[0] // ng
    part_1, part_w2 = rows_1 // na, rows_2 // na
    block = part_1 + part_w2
    width = w2.shape[1] // na
    halves = ng // 2

    def slice_of(which, put):
        first_1 = pl.multiple_of(which * rows_1, rows_1)
        first_2 = pl.multiple_of(which * rows_2, rows_2)
        t1 = mm(xt[pl.ds(first_1, rows_1), 0 : 3 * rows], dpre[...])
        t2 = mm(ht[pl.ds(first_2, rows_2), 0 : 3 * rows], grads[...])
        for i in range(na):
            put(i, t2[i * part_w2 : (i + 1) * part_w2], t1[i * part_1 : (i + 1) * part_1])

    for gh in range(halves):

        def put_send(i, low, high, gh=gh):
            core_send[gh, i, 0:part_w2] = low.astype(BF)
            core_send[gh, i, part_w2:block] = high.astype(BF)

        slice_of(2 * gh + 1 - c, put_send)
        push(core_send.at[gh], core_recv.at[gh], sem_core.at[gh], other_core, 3)
    for gh in range(halves):

        def put_own(i, low, high, gh=gh):
            total[gh, i, 0:part_w2] = low
            total[gh, i, part_w2:block] = high

        slice_of(2 * gh + c, put_own)

    a = c * x + (1 - c) * y
    b = c * y + (1 - c) * x

    def along_a(k):
        return dev(zh, c * k + (1 - c) * x, c * y + (1 - c) * k, c, g)

    def in_plane(k):
        ka, kb = div(k, na), rem(k, na)
        return dev(zh, c * ka + (1 - c) * kb, c * kb + (1 - c) * ka, c, g)

    def along_b(k):
        return dev(zh, c * x + (1 - c) * k, c * k + (1 - c) * y, c, g)

    for gh in range(halves):
        arrived(core_recv.at[gh], sem_core.at[gh])
        total[gh] = total[gh] + core_recv[gh].astype(F32)
        send_1[gh] = total[gh].astype(BF)
        for j in range(1, na):
            k = rem(a + j, na)
            push(send_1.at[gh, k], recv_1.at[gh, a], sem_1.at[gh], along_a(k), 4)
    for gh in range(halves):
        part = total[gh, a]
        arrived(recv_1.at[gh, pl.ds(0, na - 1)], sem_1.at[gh])
        for j in range(1, na):
            part = part + recv_1[gh, rem(a + j, na)].astype(F32)
        for i in range(na):
            part_2[gh, i] = part[:, i * width : (i + 1) * width]
            send_2[gh, i] = part[:, i * width : (i + 1) * width].astype(BF)
        for j in range(1, na):
            k = rem(b + j, na)
            push(send_2.at[gh, k], recv_2.at[gh, b], sem_2.at[gh], along_b(k), 5)
    matched = rem(g + c, 2) == 0
    for gh in range(halves):
        part = part_2[gh, b]
        arrived(recv_2.at[gh, pl.ds(0, na - 1)], sem_2.at[gh])
        for j in range(1, na):
            part = part + recv_2[gh, rem(b + j, na)].astype(F32)
        send_z[gh] = part.astype(BF)
        to = 2 * gh + c
        for zp in range(nzh):
            to_z = rem(zh + zp, nzh)
            elsewhere = jnp.logical_or(to_z != zh, to != g)
            target = dev(to_z, x, y, c, to)

            @pl.when(elsewhere)
            def _(gh=gh, target=target):
                push(send_z.at[gh], recv_z.at[z], sem_rz.at[0], target, 6)


    @pl.when(matched)
    def _():
        recv_z[z] = send_z[div(g, 2)]
        arrived(recv_z.at[pl.ds(0, nz - 1)], sem_rz.at[0])
        piece = jnp.zeros((block, width), F32)
        for k in range(nz):
            piece = piece + recv_z[k].astype(F32)
        slot = a * na + b
        places = na * na
        parts_sq[slot] = jnp.full((1, width), jnp.sum(piece * piece), F32)
        for t in range(1, places):
            to = in_plane(rem(slot + t, places))
            push(parts_sq.at[slot], parts_sq.at[slot], sem_q.at[0], to, 7)
        gathered[slot] = piece
        for t in range(1, places):
            to = in_plane(rem(slot + t, places))
            push(gathered.at[slot], gathered.at[slot], sem_p.at[0], to, 8)
        arrived(parts_sq.at[pl.ds(0, places - 1)], sem_q.at[0])
        ss = parts_sq[0]
        for i in range(1, places):
            ss = ss + parts_sq[i]
        squares[g] = ss
        for k in sorted(range(1 - ng // 2, ng // 2 + 1), key=abs, reverse=True):
            if k:
                to = rem(z + k + nz, nz)
                for cc in range(2):
                    target = dev(div(to, ng), x, y, cc, rem(to, ng))
                    push(squares.at[g], squares.at[g], sem_s.at[0], target, 9)
        push(squares.at[g], squares.at[g], sem_t.at[0], other_core, 9)
        arrived(gathered.at[pl.ds(0, places - 1)], sem_p.at[0])
        push(gathered, gathered, sem_c.at[0], other_core, 10)
        all_sent(7, parts_sq.at[pl.ds(0, places - 1)])
        all_sent(8, gathered.at[pl.ds(0, places - 1)])
        all_sent(9, parts_sq.at[pl.ds(0, 2 * ng - 1)])
        all_sent(10, gathered)
        all_sent(6, recv_z.at[pl.ds(0, halves * nzh - 1)])

    @pl.when(jnp.logical_not(matched))
    def _():
        arrived(squares.at[g], sem_t.at[0])
        arrived(gathered, sem_c.at[0])
        all_sent(6, recv_z.at[pl.ds(0, halves * nzh)])

    arrived(squares.at[pl.ds(0, ng - 1)], sem_s.at[0])
    ss = squares[0]
    for k in range(1, ng):
        ss = ss + squares[k]
    norm_out[...] = ss

    all_sent(0, buf_y.at[pl.ds(1, 2 * na - 1)])
    all_sent(1, buf_x.at[pl.ds(1, na - 1)])
    all_sent(2, buf_z.at[pl.ds(0, nz - 1)])
    all_sent(3, core_send)
    all_sent(4, send_1.at[pl.ds(0, halves), pl.ds(0, na - 1)])
    all_sent(5, send_2.at[pl.ds(0, halves), pl.ds(0, na - 1)])
    for cond, make in conditional:

        @pl.when(cond)
        def _(make=make):
            make().wait_send()


def finish(na, count, loss_in, pieces, squares, loss_out, g1_out, g2_out):
    low = g2_out.shape[0] // na
    high = g1_out.shape[0] // na
    width = pieces.shape[2]
    factor = jnp.minimum(1.0, math.sqrt(count) / jnp.sqrt(squares[...] + 1e-06))
    loss_out[...] = loss_in[...]
    for i in range(na):
        for k in range(na):
            column = slice(k * width, (k + 1) * width)
            g2_out[i * low : (i + 1) * low, column] = pieces[i * na + k, 0:low] * factor
            g1_out[i * high : (i + 1) * high, column] = pieces[i * na + k, low:] * factor


def per_device(dims, features, w_first, w_second, table, heads, relations, tails, negatives, partner):
    nzh, na, ng = dims
    nz = nzh * ng
    own, d_in = features.shape
    d_hid, d_enc = w_second.shape
    edges = heads.shape[1]
    rows = own * ng
    rows_1, rows_2 = d_in // ng, d_hid // ng
    block, width, halves = (rows_1 + rows_2) // na, d_enc // na, ng // 2
    lanes = max(256, 3 * rows)
    vmem = pl.BlockSpec(memory_space=pltpu.VMEM)
    hbm = pl.BlockSpec(memory_space=pltpu.HBM)
    V, S = pltpu.VMEM, pltpu.SemaphoreType.DMA
    loss, pieces, squares = pl.pallas_call(
        functools.partial(body, dims),
        out_shape=(
            jax.ShapeDtypeStruct(heads.shape, F32),
            jax.ShapeDtypeStruct((na * na, block, width), F32),
            jax.ShapeDtypeStruct((1, width), F32),
        ),
        in_specs=[hbm] * 9,
        out_specs=(vmem, vmem, vmem),
        scratch_shapes=[
            V(features.shape, BF),
            V(w_first.shape, BF),
            V(w_second.shape, BF),
            V(table.shape, BF),
            V(heads.shape, jnp.int32),
            V(relations.shape, jnp.int32),
            V(tails.shape, jnp.int32),
            V(negatives.shape, jnp.int32),
            pltpu.SMEM(partner.shape, jnp.int32),
            V((8, edges), F32),
            V((2 * na, own, d_in), BF),
            V((2, own, d_in), BF),
            V((na, 2, own, d_in), BF),
            V((nz, 2, own, d_in), BF),
            V((ng, own, d_in), BF),
            V((2, edges, d_enc), BF),
            V((2, edges, d_enc), BF),
            V((3 * rows, d_enc), BF),
            V((3 * rows, d_hid), F32),
            V((3 * rows, d_enc), BF),
            V((3 * rows, d_hid), BF),
            V((d_in, lanes), BF),
            V((d_hid, lanes), BF),
            V((halves, na, block, d_enc), BF),
            V((halves, na, block, d_enc), BF),
            V((halves, na, block, d_enc), F32),
            V((halves, na, block, d_enc), BF),
            V((halves, na, block, d_enc), BF),
            V((halves, na, block, width), F32),
            V((halves, na, block, width), BF),
            V((halves, na, block, width), BF),
            V((halves, block, width), BF),
            V((nz, block, width), BF),
            V((na * na, 1, width), F32),
            V((ng, 1, width), F32),
            S((11,)),
            S((11,)),
            S((14,)),
            S((1,)),
            S((1,)),
            S((nz, 2)),
            S((ng,)),
            S((halves,)),
            S((halves,)),
            S((halves,)),
            S((1,)),
            S((1,)),
            S((1,)),
            S((1,)),
            S((1,)),
            S((1,)),
        ],
        compiler_params=pltpu.CompilerParams(
            collective_id=0, has_side_effects=True, vmem_limit_bytes=60 * 1024 * 1024
        ),
        name="step",
    )(features, w_first, w_second, table, heads, relations, tails, negatives, partner)
    return pl.pallas_call(
        functools.partial(finish, na, float(w_first.size + w_second.size)),
        out_shape=(
            jax.ShapeDtypeStruct(heads.shape, F32),
            jax.ShapeDtypeStruct((rows_1, d_hid), F32),
            jax.ShapeDtypeStruct((rows_2, d_enc), F32),
        ),
        in_specs=[vmem] * 3,
        out_specs=(vmem, vmem, vmem),
        name="finish",
    )(loss, pieces, squares)


def solution(mesh):
    ng = mesh.shape["grp"]
    na = math.isqrt(mesh.shape["dom"] // 4)
    return jax.shard_map(
        functools.partial(per_device, (2, na, ng)),
        mesh=mesh,
        in_specs=(
            P(("dom", "grp"), None),
            P(),
            P(),
            P(),
            P(None, ("dom", "grp")),
            P(None, ("dom", "grp")),
            P(None, ("dom", "grp")),
            P(),
            P(),
        ),
        out_specs=(P(None, ("dom", "grp")), P("grp", None), P("grp", None)),
        check_vma=False,
    )
```

```python
import functools
import math

import jax
import jax.numpy as jnp
from jax import lax
from jax.experimental import pallas as pl
from jax.experimental.pallas import tpu as pltpu
from jax.sharding import PartitionSpec as P

MESH = pl.DeviceIdType.MESH
BF = jnp.bfloat16
F32 = jnp.float32
HOP = 3
NEAR = 4
STEP = 1
RELAY = {0: (4, 3, 2, 1), 4: (4, 3, 2, 1)}


def mm(a, b):
    return jnp.dot(a, b, preferred_element_type=F32)


def nt(a, b):
    return lax.dot_general(a, b, (((1,), (1,)), ((), ())), preferred_element_type=F32)


def tn(a, b):
    return lax.dot_general(a, b, (((0,), (0,)), ((), ())), preferred_element_type=F32)


def sigmoid(v):
    return 1.0 / (1.0 + jnp.exp(-v))


def softplus(v):
    return jnp.maximum(v, 0.0) + jnp.log1p(jnp.exp(-jnp.abs(v)))


def body(
    dims,
    feat_hbm,
    w1_hbm,
    w2_hbm,
    table_hbm,
    heads_hbm,
    rels_hbm,
    tails_hbm,
    negs_hbm,
    partner_hbm,
    loss_out,
    gathered,
    norm_out,
    feat,
    w1,
    w2,
    table,
    heads,
    rels,
    tails,
    negs,
    partner,
    ids,
    buf_y,
    buf_z,
    buf_o,
    rel_rows,
    query,
    enc,
    slope,
    grads,
    dpre,
    xt,
    ht,
    core_send,
    core_recv,
    send_1,
    recv_1,
    send_z,
    recv_z,
    parts_sq,
    squares,
    spare,
    load_sem,
    send_sem,
    line_sem,
    sem_y,
    sem_z,
    sem_o,
    sem_core,
    sem_1,
    sem_rz,
    sem_q,
    sem_p,
    sem_c,
    sem_s,
    sem_t,
):
    nzh, na, ng = dims
    nz = nzh * ng
    rem, div = lax.rem, lax.div
    dom = lax.axis_index("dom")
    g = lax.axis_index("grp")
    c = rem(dom, 2)
    y = rem(div(dom, 2), na)
    x = rem(div(dom, 2 * na), na)
    zh = div(dom, 2 * na * na)
    z = zh * ng + g
    bits = na.bit_length() - 1

    def dev(zh_, x_, y_, c_, g_):
        return (((zh_ * na + x_) * na + y_) * 2 + c_, g_)

    def xor(v, k):
        out = 0
        for b in range(bits):
            out = out + rem(div(v, 1 << b) + (k >> b & 1), 2) * (1 << b)
        return out

    def on_ring(step):
        to = rem(z + step + nz, nz)
        return dev(div(to, ng), x, y, c, rem(to, ng))

    other_core = dev(zh, x, y, 1 - c, g)
    conditional = []
    sent = {}

    def push(src, dst, sem, target, group):
        sent[group] = sent.get(group, 0) + 1
        pltpu.make_async_remote_copy(
            src_ref=src,
            dst_ref=dst,
            send_sem=send_sem.at[group],
            recv_sem=sem,
            device_id=target,
            device_id_type=MESH,
        ).start()

    def all_sent(group, like):
        pltpu.make_async_remote_copy(
            src_ref=like,
            dst_ref=like,
            send_sem=send_sem.at[group],
            recv_sem=sem_core.at[0],
            device_id=other_core,
            device_id_type=MESH,
        ).wait_send()

    def arrived(dst, sem):
        pltpu.make_async_remote_copy(
            src_ref=dst,
            dst_ref=dst,
            send_sem=send_sem.at[0],
            recv_sem=sem,
            device_id=other_core,
            device_id_type=MESH,
        ).wait_recv()

    def ring(buf, sem, group):
        reach = {1: nz // 2, -1: nz - 1 - nz // 2}
        waited = set()
        for base in sorted(RELAY):
            for way in (1, -1):
                if base > reach[way]:
                    continue
                source = rem(z - way * base + nz, nz)
                held, flag = buf.at[source], sem.at[source]
                if base:
                    arrived(held, flag)
                    waited.add(way * base)
                for step in RELAY[base]:
                    if base + step <= reach[way]:
                        push(held, held, flag, on_ring(way * step), group)
            yield
        for way in (1, -1):
            for dist in range(1, reach[way] + 1):
                if way * dist not in waited:
                    source = rem(z - way * dist + nz, nz)
                    arrived(buf.at[source], sem.at[source])

    def push_if(cond, *what):
        index = len(conditional)

        def make():
            src, dst, sem, target = what
            return pltpu.make_async_remote_copy(
                src_ref=src,
                dst_ref=dst,
                send_sem=line_sem.at[index],
                recv_sem=sem,
                device_id=target,
                device_id_type=MESH,
            )

        @pl.when(cond)
        def _():
            make().start()

        conditional.append((cond, make))

    def arrived_if(cond, *what):
        @pl.when(cond)
        def _():
            arrived(*what)

    def line(buf, sem):
        def within(k):
            return jnp.logical_and(k >= 0, k < ng)

        seen = set()
        for base in range(0, ng - 1, HOP):
            for way in (1, -1):
                source = g - way * base
                there = within(source)
                held = buf.at[rem(source + ng, ng)]
                flag = sem.at[rem(source + ng, ng)]
                if base:
                    arrived_if(there, held, flag)
                    seen.add(-way * base)
                for step in range(min(HOP, ng - 1 - base), 0, -1):
                    to = g + way * step
                    both = jnp.logical_and(there, within(to))
                    push_if(both, held, held, flag, dev(zh, x, y, c, rem(to + ng, ng)))
            yield
        for way in (1, -1):
            for dist in range(1, ng):
                if -way * dist not in seen:
                    source = rem(g - way * dist + ng, ng)
                    arrived_if(within(g - way * dist), buf.at[source], sem.at[source])

    barrier = pltpu.get_barrier_semaphore()
    places = na * na
    shifts = sorted(range(1, 2 * places), key=lambda k: -sum(min(v, na - v) for v in (k // (2 * na), k // 2 % na)))

    def shifted(k):
        return dev(zh, xor(x, k // (2 * na)), xor(y, k // 2 % na), rem(c + k % 2, 2), g)

    peers = [shifted(k) for k in shifts]
    near = min(NEAR, nz // 2)
    peers += [on_ring(k) for k in range(1, nz) if min(k, nz - k) <= near]
    for peer in peers:
        pl.semaphore_signal(barrier, inc=1, device_id=peer, device_id_type=MESH)

    pairs = (
        (feat_hbm, feat),
        (feat_hbm, buf_y.at[0]),
        (feat_hbm, buf_o.at[g]),
        (partner_hbm, partner),
        (heads_hbm, heads),
        (rels_hbm, rels),
        (tails_hbm, tails),
        (negs_hbm, negs),
        (table_hbm, table),
        (w1_hbm, w1),
        (w2_hbm, w2),
    )
    loads = []
    for i, (src, dst) in enumerate(pairs):
        loads.append(pltpu.make_async_copy(src, dst, load_sem.at[i]))
        loads[-1].start()
    for load in loads[0:3]:
        load.wait()
    pl.semaphore_wait(barrier, len(peers))

    for k in shifts:
        push(feat, buf_y.at[k], sem_y.at[0], shifted(k), 0)
    own_ring = line(buf_o, sem_o)
    next(own_ring)

    for load in loads[3:9]:
        load.wait()
    ids[0:2] = heads[...].astype(F32)
    ids[2:4] = rels[...].astype(F32)
    ids[4:6] = tails[...].astype(F32)
    ids[6:8] = jnp.zeros_like(ids[6:8])
    columns = jnp.transpose(ids[...])
    nrel = table.shape[0]
    edges = heads.shape[1]
    for r in range(2):
        pick = lax.broadcasted_iota(jnp.int32, (edges, nrel), 1).astype(F32) == columns[:, 2 + r : 3 + r]
        rel_rows[r] = mm(pick.astype(BF), table[...]).astype(BF)

    masks = [partner[r, 0] for r in range(2)]
    next(own_ring, None)
    arrived(buf_y.at[pl.ds(1, 2 * places - 1)], sem_y.at[0])
    for r in range(2):
        buf_z[z, r] = buf_y[masks[r] % (2 * places)]
    far_ring = ring(buf_z, sem_z, 2)
    next(far_ring)
    for _ in own_ring:
        pass

    for load in loads[9:]:
        load.wait()
    rows = 8 * ng
    half = w2.shape[1] // 2
    lane = lax.broadcasted_iota(jnp.int32, (edges, rows), 1).astype(F32)

    def encode(x_rows, first, count, at):
        pre = mm(x_rows, w1[...])
        s = sigmoid(pre)
        hidden = (pre * s).astype(BF)
        enc[first : first + count] = mm(hidden, w2[...]).astype(BF)
        slope[first : first + count] = s * (1.0 + pre * (1.0 - s))
        xt[:, at : at + count] = jnp.transpose(x_rows)
        ht[:, at : at + count] = jnp.transpose(hidden)

    own_x = buf_o[...].astype(F32).reshape(rows, feat.shape[1]).astype(BF)
    encode(own_x, 2 * rows, rows, 2 * rows)
    picks = []
    for r in range(2):
        head_pick = (lane == columns[:, r : r + 1]).astype(BF)
        picks.append(head_pick)
        head = mm(head_pick, enc[2 * rows : 3 * rows])
        rel = rel_rows[r].astype(F32)
        h_re, h_im = head[:, :half], head[:, half:]
        r_re, r_im = rel[:, :half], rel[:, half:]
        query[r, :, :half] = (h_re * r_re - h_im * r_im).astype(BF)
        query[r, :, half:] = (h_re * r_im + h_im * r_re).astype(BF)
    counts = []
    nneg = negs.shape[1]
    for r in range(2):
        hit = lax.broadcasted_iota(jnp.int32, (rows, nneg), 0) == negs[r : r + 1, :]
        counts.append(nt(jnp.ones((8, nneg), BF), hit.astype(F32).astype(BF))[0:1])
    for _ in far_ring:
        pass

    far = []
    for r in range(2):
        half_of = rem(zh + (masks[r] // (2 * places)) % 2, 2)
        rows_r = buf_z[pl.ds(half_of * ng, ng), r]
        far.append(rows_r.astype(F32).reshape(rows, feat.shape[1]))
    encode(jnp.concatenate(far, axis=0).astype(BF), 0, 2 * rows, 0)

    own = None
    losses = []
    for r in range(2):
        other = enc[r * rows : (r + 1) * rows]
        q = query[r]
        score = nt(q, other)
        tail_pick = jnp.where(lane == columns[:, 4 + r : 5 + r], 1.0, 0.0)
        positive = jnp.sum(score * tail_pick, axis=1, keepdims=True)
        losses.append(
            softplus(-positive) + jnp.sum(softplus(score) * counts[r], axis=1, keepdims=True) / nneg
        )
        weight_neg = (sigmoid(score) / nneg).astype(BF).astype(F32)
        weight_pos = -sigmoid(-positive)
        weight = (weight_neg * counts[r] + tail_pick * weight_pos).astype(BF)
        d_query = mm(weight, other)
        grads[r * rows : (r + 1) * rows] = tn(weight, q).astype(BF)
        rel = rel_rows[r].astype(F32)
        q_re, q_im = d_query[:, :half], d_query[:, half:]
        r_re, r_im = rel[:, :half], rel[:, half:]
        d_head = jnp.concatenate([q_re * r_re + q_im * r_im, q_im * r_re - q_re * r_im], axis=1)
        term = tn(picks[r], d_head.astype(BF))
        own = term if own is None else own + term
    grads[2 * rows : 3 * rows] = own.astype(BF)
    wide = lax.broadcasted_iota(jnp.int32, (edges, 128), 1)
    both = jnp.where(wide == 0, losses[0], jnp.where(wide == 1, losses[1], 0.0))
    loss_out[...] = jnp.transpose(both)[0:2]

    dpre[...] = (nt(grads[...], w2[...]) * slope[...]).astype(BF)
    rows_1, rows_2 = w1.shape[0] // ng, w2.shape[0] // ng
    part_1, part_w2 = rows_1 // na, rows_2 // na
    block = part_1 + part_w2
    width = w2.shape[1] // na
    halves = ng // 2

    def slice_of(which, put):
        first_1 = pl.multiple_of(which * rows_1, rows_1)
        first_2 = pl.multiple_of(which * rows_2, rows_2)
        t1 = mm(xt[pl.ds(first_1, rows_1), 0 : 3 * rows], dpre[...])
        t2 = mm(ht[pl.ds(first_2, rows_2), 0 : 3 * rows], grads[...])
        for i in range(na):
            put(i, t2[i * part_w2 : (i + 1) * part_w2], t1[i * part_1 : (i + 1) * part_1])

    for gh in range(halves):

        def put_send(i, low, high, gh=gh):
            core_send[gh, i, 0:part_w2] = low.astype(BF)
            core_send[gh, i, part_w2:block] = high.astype(BF)

        slice_of(2 * gh + 1 - c, put_send)
        push(core_send.at[gh], core_recv.at[gh], sem_core.at[gh], other_core, 3)
    a = c * x + (1 - c) * y
    b = c * y + (1 - c) * x
    slot = a * na + b
    ways = sorted(range(1, places), key=lambda k: -sum(min(v, na - v) for v in (k // na, k % na)))

    def in_plane(k):
        ka, kb = div(k, na), rem(k, na)
        return dev(zh, c * ka + (1 - c) * kb, c * kb + (1 - c) * ka, c, g)

    def turned(k):
        return rem(a + k // na, na) * na + rem(b + k % na, na)

    for first in range(0, halves, STEP):
        for gh in range(first, min(first + STEP, halves)):
            local = []
            slice_of(2 * gh + c, lambda i, low, high: local.append((low, high)))
            arrived(core_recv.at[gh], sem_core.at[gh])
            for i, (low, high) in enumerate(local):
                low = (low + core_recv[gh, i, 0:part_w2].astype(F32)).astype(BF)
                high = (high + core_recv[gh, i, part_w2:block].astype(F32)).astype(BF)
                for k in range(na):
                    column = slice(k * width, (k + 1) * width)
                    send_1[i * na + k, gh, 0:part_w2] = low[:, column]
                    send_1[i * na + k, gh, part_w2:block] = high[:, column]
        some = pl.ds(first, min(STEP, halves - first))
        for k in ways:
            to = turned(k)
            push(send_1.at[to, some], recv_1.at[slot, some], sem_1.at[first], in_plane(to), 4)
        recv_1[slot, some] = send_1[slot, some]
    matched = rem(g + c, 2) == 0
    for gh in range(halves):
        if gh % STEP == 0:
            some = pl.ds(gh, min(STEP, halves - gh))
            arrived(recv_1.at[pl.ds(0, places - 1), some], sem_1.at[gh])
        part = recv_1[0, gh].astype(F32)
        for k in range(1, places):
            part = part + recv_1[k, gh].astype(F32)
        send_z[gh] = part.astype(BF)
        to = 2 * gh + c
        for zp in range(nzh):
            to_z = rem(zh + zp, nzh)
            elsewhere = jnp.logical_or(to_z != zh, to != g)
            target = dev(to_z, x, y, c, to)

            @pl.when(elsewhere)
            def _(gh=gh, target=target):
                push(send_z.at[gh], recv_z.at[z], sem_rz.at[0], target, 6)


    @pl.when(matched)
    def _():
        recv_z[z] = send_z[div(g, 2)]
        arrived(recv_z.at[pl.ds(0, nz - 1)], sem_rz.at[0])
        piece = jnp.zeros((block, width), F32)
        for k in range(nz):
            piece = piece + recv_z[k].astype(F32)
        squares[g] = jnp.full((1, width), jnp.sum(piece * piece), F32)
        for k in sorted(range(1 - ng // 2, ng // 2 + 1), key=abs, reverse=True):
            if k:
                to = rem(z + k + nz, nz)
                target = dev(div(to, ng), x, y, rem(c + k + nz, 2), rem(to, ng))
                push(squares.at[g], squares.at[g], sem_s.at[0], target, 7)
        gathered[slot] = piece.astype(BF)
        for k in ways:
            push(gathered.at[slot], gathered.at[slot], sem_p.at[0], in_plane(turned(k)), 8)
        arrived(squares.at[pl.ds(0, ng - 1)], sem_s.at[0])
        ss = squares[0]
        for k in range(1, ng):
            ss = ss + squares[k]
        parts_sq[slot] = ss
        for k in ways:
            for cc in range(2):
                ka, kb = div(turned(k), na), rem(turned(k), na)
                target = dev(zh, c * ka + (1 - c) * kb, c * kb + (1 - c) * ka, cc, g)
                push(parts_sq.at[slot], parts_sq.at[slot], sem_q.at[0], target, 9)
        push(parts_sq.at[slot], parts_sq.at[slot], sem_t.at[0], other_core, 10)
        arrived(gathered.at[pl.ds(0, places - 1)], sem_p.at[0])
        push(gathered, gathered, sem_c.at[0], other_core, 11)
        all_sent(7, squares.at[pl.ds(0, ng - 1)])
        all_sent(8, gathered.at[pl.ds(0, places - 1)])
        all_sent(9, spare)
        all_sent(10, parts_sq.at[0])
        all_sent(11, gathered)
        all_sent(6, recv_z.at[pl.ds(0, halves * nzh - 1)])

    @pl.when(jnp.logical_not(matched))
    def _():
        arrived(parts_sq.at[0], sem_t.at[0])
        arrived(gathered, sem_c.at[0])
        all_sent(6, recv_z.at[pl.ds(0, halves * nzh)])

    arrived(parts_sq.at[pl.ds(0, places - 1)], sem_q.at[0])
    ss = parts_sq[0]
    for k in range(1, places):
        ss = ss + parts_sq[k]
    norm_out[...] = ss

    all_sent(0, buf_y.at[pl.ds(1, 2 * places - 1)])
    all_sent(2, buf_z.at[pl.ds(0, nz - 1)])
    all_sent(3, core_send)
    all_sent(4, send_1.at[pl.ds(0, places - 1)])
    for cond, make in conditional:

        @pl.when(cond)
        def _(make=make):
            make().wait_send()


def finish(na, count, loss_in, pieces, squares, loss_out, g1_out, g2_out):
    low = g2_out.shape[0] // na
    high = g1_out.shape[0] // na
    width = pieces.shape[2]
    factor = jnp.minimum(1.0, math.sqrt(count) / jnp.sqrt(squares[...] + 1e-06))
    loss_out[...] = loss_in[...]
    for i in range(na):
        for k in range(na):
            column = slice(k * width, (k + 1) * width)
            g2_out[i * low : (i + 1) * low, column] = pieces[i * na + k, 0:low].astype(F32) * factor
            g1_out[i * high : (i + 1) * high, column] = pieces[i * na + k, low:].astype(F32) * factor


def per_device(dims, features, w_first, w_second, table, heads, relations, tails, negatives, partner):
    nzh, na, ng = dims
    nz = nzh * ng
    own, d_in = features.shape
    d_hid, d_enc = w_second.shape
    edges = heads.shape[1]
    rows = own * ng
    rows_1, rows_2 = d_in // ng, d_hid // ng
    block, width, halves = (rows_1 + rows_2) // na, d_enc // na, ng // 2
    lanes = max(256, 3 * rows)
    vmem = pl.BlockSpec(memory_space=pltpu.VMEM)
    hbm = pl.BlockSpec(memory_space=pltpu.HBM)
    V, S = pltpu.VMEM, pltpu.SemaphoreType.DMA
    loss, pieces, squares = pl.pallas_call(
        functools.partial(body, dims),
        out_shape=(
            jax.ShapeDtypeStruct(heads.shape, F32),
            jax.ShapeDtypeStruct((na * na, block, width), BF),
            jax.ShapeDtypeStruct((1, width), F32),
        ),
        in_specs=[hbm] * 9,
        out_specs=(vmem, vmem, vmem),
        scratch_shapes=[
            V(features.shape, BF),
            V(w_first.shape, BF),
            V(w_second.shape, BF),
            V(table.shape, BF),
            V(heads.shape, jnp.int32),
            V(relations.shape, jnp.int32),
            V(tails.shape, jnp.int32),
            V(negatives.shape, jnp.int32),
            pltpu.SMEM(partner.shape, jnp.int32),
            V((8, edges), F32),
            V((2 * na * na, own, d_in), BF),
            V((nz, 2, own, d_in), BF),
            V((ng, own, d_in), BF),
            V((2, edges, d_enc), BF),
            V((2, edges, d_enc), BF),
            V((3 * rows, d_enc), BF),
            V((3 * rows, d_hid), F32),
            V((3 * rows, d_enc), BF),
            V((3 * rows, d_hid), BF),
            V((d_in, lanes), BF),
            V((d_hid, lanes), BF),
            V((halves, na, block, d_enc), BF),
            V((halves, na, block, d_enc), BF),
            V((na * na, halves, block, width), BF),
            V((na * na, halves, block, width), BF),
            V((halves, block, width), BF),
            V((nz, block, width), BF),
            V((na * na, 1, width), F32),
            V((ng, 1, width), F32),
            V((2 * na * na - 2, 1, width), F32),
            S((11,)),
            S((12,)),
            S((14,)),
            S((1,)),
            S((nz,)),
            S((ng,)),
            S((halves,)),
            S((halves,)),
            S((1,)),
            S((1,)),
            S((1,)),
            S((1,)),
            S((1,)),
            S((1,)),
        ],
        compiler_params=pltpu.CompilerParams(
            collective_id=0, has_side_effects=True, vmem_limit_bytes=60 * 1024 * 1024
        ),
        name="step",
    )(features, w_first, w_second, table, heads, relations, tails, negatives, partner)
    return pl.pallas_call(
        functools.partial(finish, na, float(w_first.size + w_second.size)),
        out_shape=(
            jax.ShapeDtypeStruct(heads.shape, F32),
            jax.ShapeDtypeStruct((rows_1, d_hid), F32),
            jax.ShapeDtypeStruct((rows_2, d_enc), F32),
        ),
        in_specs=[vmem] * 3,
        out_specs=(vmem, vmem, vmem),
        name="finish",
    )(loss, pieces, squares)


def solution(mesh):
    ng = mesh.shape["grp"]
    na = math.isqrt(mesh.shape["dom"] // 4)
    return jax.shard_map(
        functools.partial(per_device, (2, na, ng)),
        mesh=mesh,
        in_specs=(
            P(("dom", "grp"), None),
            P(),
            P(),
            P(),
            P(None, ("dom", "grp")),
            P(None, ("dom", "grp")),
            P(None, ("dom", "grp")),
            P(),
            P(),
        ),
        out_specs=(P(None, ("dom", "grp")), P("grp", None), P("grp", None)),
        check_vma=False,
    )
```

```python
import functools
import math

import jax
import jax.numpy as jnp
from jax import lax
from jax.experimental import pallas as pl
from jax.experimental.pallas import tpu as pltpu
from jax.sharding import PartitionSpec as P

MESH = pl.DeviceIdType.MESH
BF = jnp.bfloat16
F32 = jnp.float32
HOP = 4
NEAR = 4
STEP = 1
RELAY = {0: (4, 3, 2, 1), 4: (4, 3, 2, 1)}


def mm(a, b):
    return jnp.dot(a, b, preferred_element_type=F32)


def nt(a, b):
    return lax.dot_general(a, b, (((1,), (1,)), ((), ())), preferred_element_type=F32)


def tn(a, b):
    return lax.dot_general(a, b, (((0,), (0,)), ((), ())), preferred_element_type=F32)


def sigmoid(v):
    return 1.0 / (1.0 + jnp.exp(-v))


def softplus(v):
    return jnp.maximum(v, 0.0) + jnp.log1p(jnp.exp(-jnp.abs(v)))


def body(
    dims,
    feat_hbm,
    w1_hbm,
    w2_hbm,
    table_hbm,
    heads_hbm,
    rels_hbm,
    tails_hbm,
    negs_hbm,
    partner_hbm,
    loss_hbm,
    pieces_hbm,
    norm_hbm,
    loss_out,
    gathered,
    norm_out,
    feat,
    w1,
    w2,
    table,
    heads,
    rels,
    tails,
    negs,
    partner,
    ids,
    buf_y,
    buf_z,
    buf_o,
    rel_rows,
    query,
    enc,
    slope,
    grads,
    dpre,
    xt,
    ht,
    core_send,
    core_recv,
    send_1,
    recv_1,
    send_z,
    recv_z,
    parts_sq,
    squares,
    spare,
    out_sem,
    load_sem,
    send_sem,
    line_sem,
    sem_y,
    sem_z,
    sem_o,
    sem_core,
    sem_1,
    sem_rz,
    sem_q,
    sem_p,
    sem_c,
    sem_s,
    sem_t,
):
    nzh, na, ng = dims
    nz = nzh * ng
    rem, div = lax.rem, lax.div
    dom = lax.axis_index("dom")
    g = lax.axis_index("grp")
    c = rem(dom, 2)
    y = rem(div(dom, 2), na)
    x = rem(div(dom, 2 * na), na)
    zh = div(dom, 2 * na * na)
    z = zh * ng + g
    bits = na.bit_length() - 1

    def dev(zh_, x_, y_, c_, g_):
        return (((zh_ * na + x_) * na + y_) * 2 + c_, g_)

    def xor(v, k):
        out = 0
        for b in range(bits):
            out = out + rem(div(v, 1 << b) + (k >> b & 1), 2) * (1 << b)
        return out

    def on_ring(step):
        to = rem(z + step + nz, nz)
        return dev(div(to, ng), x, y, c, rem(to, ng))

    other_core = dev(zh, x, y, 1 - c, g)
    conditional = []
    sent = {}

    def push(src, dst, sem, target, group):
        sent[group] = sent.get(group, 0) + 1
        pltpu.make_async_remote_copy(
            src_ref=src,
            dst_ref=dst,
            send_sem=send_sem.at[group],
            recv_sem=sem,
            device_id=target,
            device_id_type=MESH,
        ).start()

    def all_sent(group, like):
        pltpu.make_async_remote_copy(
            src_ref=like,
            dst_ref=like,
            send_sem=send_sem.at[group],
            recv_sem=sem_core.at[0],
            device_id=other_core,
            device_id_type=MESH,
        ).wait_send()

    def arrived(dst, sem):
        pltpu.make_async_remote_copy(
            src_ref=dst,
            dst_ref=dst,
            send_sem=send_sem.at[0],
            recv_sem=sem,
            device_id=other_core,
            device_id_type=MESH,
        ).wait_recv()

    def ring(buf, sem, group):
        far = nz // 2
        waited = set()
        for base in sorted(RELAY):
            for way in (1, -1):
                if base >= far:
                    continue
                source = rem(z - way * base + nz, nz)
                held, flag = buf.at[source], sem.at[source]
                if base:
                    arrived(held, flag)
                    waited.add(way * base)
                for step in RELAY[base]:
                    if base + step < far:
                        push(held, held, flag, on_ring(way * step), group)
                    elif base + step == far:
                        part = held.at[(1 - way) // 2]
                        push(part, part, flag, on_ring(way * step), group)
            yield
        for dist in range(1, far + 1):
            for way in (1, -1):
                if way * dist not in waited and (way == 1 or dist < far):
                    source = rem(z - way * dist + nz, nz)
                    arrived(buf.at[source], sem.at[source])

    def push_if(cond, *what):
        index = len(conditional)

        def make():
            src, dst, sem, target = what
            return pltpu.make_async_remote_copy(
                src_ref=src,
                dst_ref=dst,
                send_sem=line_sem.at[index],
                recv_sem=sem,
                device_id=target,
                device_id_type=MESH,
            )

        @pl.when(cond)
        def _():
            make().start()

        conditional.append((cond, make))

    def arrived_if(cond, *what):
        @pl.when(cond)
        def _():
            arrived(*what)

    def line(buf, sem):
        def within(k):
            return jnp.logical_and(k >= 0, k < ng)

        seen = set()
        for base in range(0, ng - 1, HOP):
            for way in (1, -1):
                source = g - way * base
                there = within(source)
                held = buf.at[rem(source + ng, ng)]
                flag = sem.at[rem(source + ng, ng)]
                if base:
                    arrived_if(there, held, flag)
                    seen.add(-way * base)
                for step in range(min(HOP, ng - 1 - base), 0, -1):
                    to = g + way * step
                    both = jnp.logical_and(there, within(to))
                    push_if(both, held, held, flag, dev(zh, x, y, c, rem(to + ng, ng)))
            yield
        for way in (1, -1):
            for dist in range(1, ng):
                if -way * dist not in seen:
                    source = rem(g - way * dist + ng, ng)
                    arrived_if(within(g - way * dist), buf.at[source], sem.at[source])

    barrier = pltpu.get_barrier_semaphore()
    places = na * na
    shifts = sorted(range(1, 2 * places), key=lambda k: -sum(min(v, na - v) for v in (k // (2 * na), k // 2 % na)))

    def shifted(k):
        return dev(zh, xor(x, k // (2 * na)), xor(y, k // 2 % na), rem(c + k % 2, 2), g)

    peers = [shifted(k) for k in shifts]
    near = min(NEAR, nz // 2)
    peers += [on_ring(k) for k in range(1, nz) if min(k, nz - k) <= near]
    for peer in peers:
        pl.semaphore_signal(barrier, inc=1, device_id=peer, device_id_type=MESH)

    pairs = (
        (feat_hbm, feat),
        (feat_hbm, buf_y.at[0]),
        (feat_hbm, buf_o.at[g]),
        (partner_hbm, partner),
        (heads_hbm, heads),
        (rels_hbm, rels),
        (tails_hbm, tails),
        (negs_hbm, negs),
        (table_hbm, table),
        (w1_hbm, w1),
        (w2_hbm, w2),
    )
    loads = []
    for i, (src, dst) in enumerate(pairs):
        loads.append(pltpu.make_async_copy(src, dst, load_sem.at[i]))
        loads[-1].start()
    for load in loads[0:3]:
        load.wait()
    pl.semaphore_wait(barrier, len(peers))

    for k in shifts:
        push(feat, buf_y.at[k], sem_y.at[0], shifted(k), 0)
    own_ring = line(buf_o, sem_o)
    next(own_ring)

    for load in loads[3:9]:
        load.wait()
    ids[0:2] = heads[...].astype(F32)
    ids[2:4] = rels[...].astype(F32)
    ids[4:6] = tails[...].astype(F32)
    ids[6:8] = jnp.zeros_like(ids[6:8])
    columns = jnp.transpose(ids[...])
    nrel = table.shape[0]
    edges = heads.shape[1]
    for r in range(2):
        pick = lax.broadcasted_iota(jnp.int32, (edges, nrel), 1).astype(F32) == columns[:, 2 + r : 3 + r]
        rel_rows[r] = mm(pick.astype(BF), table[...]).astype(BF)

    masks = [partner[r, 0] for r in range(2)]
    next(own_ring, None)
    arrived(buf_y.at[pl.ds(1, 2 * places - 1)], sem_y.at[0])
    for r in range(2):
        buf_z[z, r] = buf_y[masks[r] % (2 * places)]
    far_ring = ring(buf_z, sem_z, 2)
    next(far_ring)
    next(far_ring)
    for _ in own_ring:
        pass

    for load in loads[9:]:
        load.wait()
    rows = 8 * ng
    half = w2.shape[1] // 2
    lane = lax.broadcasted_iota(jnp.int32, (edges, rows), 1).astype(F32)

    def encode(x_rows, first, count, at):
        pre = mm(x_rows, w1[...])
        s = sigmoid(pre)
        hidden = (pre * s).astype(BF)
        enc[first : first + count] = mm(hidden, w2[...]).astype(BF)
        slope[first : first + count] = s * (1.0 + pre * (1.0 - s))
        xt[:, at : at + count] = jnp.transpose(x_rows)
        ht[:, at : at + count] = jnp.transpose(hidden)

    own_x = buf_o[...].astype(F32).reshape(rows, feat.shape[1]).astype(BF)
    encode(own_x, 2 * rows, rows, 2 * rows)
    picks = []
    for r in range(2):
        head_pick = (lane == columns[:, r : r + 1]).astype(BF)
        picks.append(head_pick)
        head = mm(head_pick, enc[2 * rows : 3 * rows])
        rel = rel_rows[r].astype(F32)
        h_re, h_im = head[:, :half], head[:, half:]
        r_re, r_im = rel[:, :half], rel[:, half:]
        query[r, :, :half] = (h_re * r_re - h_im * r_im).astype(BF)
        query[r, :, half:] = (h_re * r_im + h_im * r_re).astype(BF)
    counts = []
    nneg = negs.shape[1]
    for r in range(2):
        hit = lax.broadcasted_iota(jnp.int32, (rows, nneg), 0) == negs[r : r + 1, :]
        counts.append(nt(jnp.ones((8, nneg), BF), hit.astype(F32).astype(BF))[0:1])
    for _ in far_ring:
        pass

    far = []
    for r in range(2):
        half_of = rem(zh + (masks[r] // (2 * places)) % 2, 2)
        rows_r = buf_z[pl.ds(half_of * ng, ng), r]
        far.append(rows_r.astype(F32).reshape(rows, feat.shape[1]))
    encode(jnp.concatenate(far, axis=0).astype(BF), 0, 2 * rows, 0)

    own = None
    losses = []
    for r in range(2):
        other = enc[r * rows : (r + 1) * rows]
        q = query[r]
        score = nt(q, other)
        tail_pick = jnp.where(lane == columns[:, 4 + r : 5 + r], 1.0, 0.0)
        positive = jnp.sum(score * tail_pick, axis=1, keepdims=True)
        losses.append(
            softplus(-positive) + jnp.sum(softplus(score) * counts[r], axis=1, keepdims=True) / nneg
        )
        weight_neg = (sigmoid(score) / nneg).astype(BF).astype(F32)
        weight_pos = -sigmoid(-positive)
        weight = (weight_neg * counts[r] + tail_pick * weight_pos).astype(BF)
        d_query = mm(weight, other)
        grads[r * rows : (r + 1) * rows] = tn(weight, q).astype(BF)
        rel = rel_rows[r].astype(F32)
        q_re, q_im = d_query[:, :half], d_query[:, half:]
        r_re, r_im = rel[:, :half], rel[:, half:]
        d_head = jnp.concatenate([q_re * r_re + q_im * r_im, q_im * r_re - q_re * r_im], axis=1)
        term = tn(picks[r], d_head.astype(BF))
        own = term if own is None else own + term
    grads[2 * rows : 3 * rows] = own.astype(BF)
    wide = lax.broadcasted_iota(jnp.int32, (edges, 128), 1)
    both = jnp.where(wide == 0, losses[0], jnp.where(wide == 1, losses[1], 0.0))
    loss_out[...] = jnp.transpose(both)[0:2]
    outs = [
        pltpu.make_async_copy(loss_out, loss_hbm, out_sem.at[0]),
        pltpu.make_async_copy(gathered, pieces_hbm, out_sem.at[1]),
        pltpu.make_async_copy(norm_out, norm_hbm, out_sem.at[2]),
    ]
    outs[0].start()

    dpre[...] = (nt(grads[...], w2[...]) * slope[...]).astype(BF)
    rows_1, rows_2 = w1.shape[0] // ng, w2.shape[0] // ng
    part_1, part_w2 = rows_1 // na, rows_2 // na
    block = part_1 + part_w2
    width = w2.shape[1] // na
    halves = ng // 2

    def slice_of(which, put):
        first_1 = pl.multiple_of(which * rows_1, rows_1)
        first_2 = pl.multiple_of(which * rows_2, rows_2)
        t1 = mm(xt[pl.ds(first_1, rows_1), 0 : 3 * rows], dpre[...])
        t2 = mm(ht[pl.ds(first_2, rows_2), 0 : 3 * rows], grads[...])
        for i in range(na):
            put(i, t2[i * part_w2 : (i + 1) * part_w2], t1[i * part_1 : (i + 1) * part_1])

    for gh in range(halves):

        def put_send(i, low, high, gh=gh):
            core_send[gh, i, 0:part_w2] = low.astype(BF)
            core_send[gh, i, part_w2:block] = high.astype(BF)

        slice_of(2 * gh + 1 - c, put_send)
        push(core_send.at[gh], core_recv.at[gh], sem_core.at[gh], other_core, 3)
    a = c * x + (1 - c) * y
    b = c * y + (1 - c) * x
    slot = a * na + b
    ways = sorted(range(1, places), key=lambda k: -sum(min(v, na - v) for v in (k // na, k % na)))

    def in_plane(k):
        ka, kb = div(k, na), rem(k, na)
        return dev(zh, c * ka + (1 - c) * kb, c * kb + (1 - c) * ka, c, g)

    def turned(k):
        return rem(a + k // na, na) * na + rem(b + k % na, na)

    for first in range(0, halves, STEP):
        for gh in range(first, min(first + STEP, halves)):
            local = []
            slice_of(2 * gh + c, lambda i, low, high: local.append((low, high)))
            arrived(core_recv.at[gh], sem_core.at[gh])
            for i, (low, high) in enumerate(local):
                low = (low + core_recv[gh, i, 0:part_w2].astype(F32)).astype(BF)
                high = (high + core_recv[gh, i, part_w2:block].astype(F32)).astype(BF)
                for k in range(na):
                    column = slice(k * width, (k + 1) * width)
                    send_1[i * na + k, gh, 0:part_w2] = low[:, column]
                    send_1[i * na + k, gh, part_w2:block] = high[:, column]
        some = pl.ds(first, min(STEP, halves - first))
        for k in ways:
            to = turned(k)
            push(send_1.at[to, some], recv_1.at[slot, some], sem_1.at[first], in_plane(to), 4)
        recv_1[slot, some] = send_1[slot, some]
    matched = rem(g + c, 2) == 0
    for gh in range(halves):
        if gh % STEP == 0:
            some = pl.ds(gh, min(STEP, halves - gh))
            arrived(recv_1.at[pl.ds(0, places - 1), some], sem_1.at[gh])
        part = recv_1[0, gh].astype(F32)
        for k in range(1, places):
            part = part + recv_1[k, gh].astype(F32)
        send_z[gh] = part.astype(BF)
        to = 2 * gh + c
        for zp in range(nzh):
            to_z = rem(zh + zp, nzh)
            elsewhere = jnp.logical_or(to_z != zh, to != g)
            target = dev(to_z, x, y, c, to)

            @pl.when(elsewhere)
            def _(gh=gh, target=target):
                push(send_z.at[gh], recv_z.at[z], sem_rz.at[0], target, 6)


    @pl.when(matched)
    def _():
        recv_z[z] = send_z[div(g, 2)]
        arrived(recv_z.at[pl.ds(0, nz - 1)], sem_rz.at[0])
        piece = jnp.zeros((block, width), F32)
        for k in range(nz):
            piece = piece + recv_z[k].astype(F32)
        squares[g] = jnp.full((1, width), jnp.sum(piece * piece), F32)
        for k in sorted(range(1 - ng // 2, ng // 2 + 1), key=abs, reverse=True):
            if k:
                to = rem(z + k + nz, nz)
                target = dev(div(to, ng), x, y, rem(c + k + nz, 2), rem(to, ng))
                push(squares.at[g], squares.at[g], sem_s.at[0], target, 7)
        gathered[slot] = piece.astype(BF)
        for k in ways:
            push(gathered.at[slot], gathered.at[slot], sem_p.at[0], in_plane(turned(k)), 8)
        arrived(squares.at[pl.ds(0, ng - 1)], sem_s.at[0])
        ss = squares[0]
        for k in range(1, ng):
            ss = ss + squares[k]
        parts_sq[slot] = ss
        for k in ways:
            for cc in range(2):
                ka, kb = div(turned(k), na), rem(turned(k), na)
                target = dev(zh, c * ka + (1 - c) * kb, c * kb + (1 - c) * ka, cc, g)
                push(parts_sq.at[slot], parts_sq.at[slot], sem_q.at[0], target, 9)
        push(parts_sq.at[slot], parts_sq.at[slot], sem_t.at[0], other_core, 10)
        arrived(gathered.at[pl.ds(0, places - 1)], sem_p.at[0])
        push(gathered, gathered, sem_c.at[0], other_core, 11)
        outs[1].start()
        all_sent(7, squares.at[pl.ds(0, ng - 1)])
        all_sent(8, gathered.at[pl.ds(0, places - 1)])
        all_sent(9, spare)
        all_sent(10, parts_sq.at[0])
        all_sent(11, gathered)
        all_sent(6, recv_z.at[pl.ds(0, halves * nzh - 1)])

    @pl.when(jnp.logical_not(matched))
    def _():
        arrived(parts_sq.at[0], sem_t.at[0])
        arrived(gathered, sem_c.at[0])
        outs[1].start()
        all_sent(6, recv_z.at[pl.ds(0, halves * nzh)])

    arrived(parts_sq.at[pl.ds(0, places - 1)], sem_q.at[0])
    ss = parts_sq[0]
    for k in range(1, places):
        ss = ss + parts_sq[k]
    norm_out[...] = ss
    outs[2].start()

    all_sent(0, buf_y.at[pl.ds(1, 2 * places - 1)])
    all_sent(2, buf_z.at[pl.ds(0, nz - 1)])
    all_sent(3, core_send)
    all_sent(4, send_1.at[pl.ds(0, places - 1)])
    for cond, make in conditional:

        @pl.when(cond)
        def _(make=make):
            make().wait_send()

    for copy in outs:
        copy.wait()


def finish(na, count, *refs):
    loss_hbm, pieces_hbm, squares_hbm, loss_out, g1_hbm, g2_hbm = refs[:6]
    pieces, squares, g1_out, g2_out, sem = refs[6:]
    into = [
        pltpu.make_async_copy(pieces_hbm, pieces, sem.at[0]),
        pltpu.make_async_copy(squares_hbm, squares, sem.at[1]),
        pltpu.make_async_copy(loss_hbm, loss_out, sem.at[2]),
    ]
    for copy in into:
        copy.start()
    low = g2_out.shape[0] // na
    high = g1_out.shape[0] // na
    width = pieces.shape[2]
    for copy in into[:2]:
        copy.wait()
    factor = jnp.minimum(1.0, math.sqrt(count) / jnp.sqrt(squares[...] + 1e-06))
    for i in range(na):
        for k in range(na):
            column = slice(k * width, (k + 1) * width)
            g2_out[i * low : (i + 1) * low, column] = pieces[i * na + k, 0:low].astype(F32) * factor
            g1_out[i * high : (i + 1) * high, column] = pieces[i * na + k, low:].astype(F32) * factor
    out = [
        pltpu.make_async_copy(g1_out, g1_hbm, sem.at[3]),
        pltpu.make_async_copy(g2_out, g2_hbm, sem.at[4]),
    ]
    for copy in out:
        copy.start()
    into[2].wait()
    for copy in out:
        copy.wait()


def per_device(dims, features, w_first, w_second, table, heads, relations, tails, negatives, partner):
    nzh, na, ng = dims
    nz = nzh * ng
    own, d_in = features.shape
    d_hid, d_enc = w_second.shape
    edges = heads.shape[1]
    rows = own * ng
    rows_1, rows_2 = d_in // ng, d_hid // ng
    block, width, halves = (rows_1 + rows_2) // na, d_enc // na, ng // 2
    lanes = max(256, 3 * rows)
    vmem = pl.BlockSpec(memory_space=pltpu.VMEM)
    hbm = pl.BlockSpec(memory_space=pltpu.HBM)
    V, S = pltpu.VMEM, pltpu.SemaphoreType.DMA
    loss, pieces, squares = pl.pallas_call(
        functools.partial(body, dims),
        out_shape=(
            jax.ShapeDtypeStruct(heads.shape, F32),
            jax.ShapeDtypeStruct((na * na, block, width), BF),
            jax.ShapeDtypeStruct((1, width), F32),
        ),
        in_specs=[hbm] * 9,
        out_specs=(hbm, hbm, hbm),
        scratch_shapes=[
            V(heads.shape, F32),
            V((na * na, block, width), BF),
            V((1, width), F32),
            V(features.shape, BF),
            V(w_first.shape, BF),
            V(w_second.shape, BF),
            V(table.shape, BF),
            V(heads.shape, jnp.int32),
            V(relations.shape, jnp.int32),
            V(tails.shape, jnp.int32),
            V(negatives.shape, jnp.int32),
            pltpu.SMEM(partner.shape, jnp.int32),
            V((8, edges), F32),
            V((2 * na * na, own, d_in), BF),
            V((nz, 2, own, d_in), BF),
            V((ng, own, d_in), BF),
            V((2, edges, d_enc), BF),
            V((2, edges, d_enc), BF),
            V((3 * rows, d_enc), BF),
            V((3 * rows, d_hid), F32),
            V((3 * rows, d_enc), BF),
            V((3 * rows, d_hid), BF),
            V((d_in, lanes), BF),
            V((d_hid, lanes), BF),
            V((halves, na, block, d_enc), BF),
            V((halves, na, block, d_enc), BF),
            V((na * na, halves, block, width), BF),
            V((na * na, halves, block, width), BF),
            V((halves, block, width), BF),
            V((nz, block, width), BF),
            V((na * na, 1, width), F32),
            V((ng, 1, width), F32),
            V((2 * na * na - 2, 1, width), F32),
            S((3,)),
            S((11,)),
            S((12,)),
            S((14,)),
            S((1,)),
            S((nz,)),
            S((ng,)),
            S((halves,)),
            S((halves,)),
            S((1,)),
            S((1,)),
            S((1,)),
            S((1,)),
            S((1,)),
            S((1,)),
        ],
        compiler_params=pltpu.CompilerParams(
            collective_id=0, has_side_effects=True, vmem_limit_bytes=60 * 1024 * 1024
        ),
        name="step",
    )(features, w_first, w_second, table, heads, relations, tails, negatives, partner)
    return pl.pallas_call(
        functools.partial(finish, na, float(w_first.size + w_second.size)),
        out_shape=(
            jax.ShapeDtypeStruct(heads.shape, F32),
            jax.ShapeDtypeStruct((rows_1, d_hid), F32),
            jax.ShapeDtypeStruct((rows_2, d_enc), F32),
        ),
        in_specs=[hbm] * 3,
        out_specs=(vmem, hbm, hbm),
        scratch_shapes=[
            V((na * na, block, width), BF),
            V((1, width), F32),
            V((rows_1, d_hid), F32),
            V((rows_2, d_enc), F32),
            S((5,)),
        ],
        compiler_params=pltpu.CompilerParams(vmem_limit_bytes=60 * 1024 * 1024),
        name="finish",
    )(loss, pieces, squares)


def solution(mesh):
    ng = mesh.shape["grp"]
    na = math.isqrt(mesh.shape["dom"] // 4)
    return jax.shard_map(
        functools.partial(per_device, (2, na, ng)),
        mesh=mesh,
        in_specs=(
            P(("dom", "grp"), None),
            P(),
            P(),
            P(),
            P(None, ("dom", "grp")),
            P(None, ("dom", "grp")),
            P(None, ("dom", "grp")),
            P(),
            P(),
        ),
        out_specs=(P(None, ("dom", "grp")), P("grp", None), P("grp", None)),
        check_vma=False,
    )
```

```python
import functools
import math

import jax
import jax.numpy as jnp
from jax import lax
from jax.experimental import pallas as pl
from jax.experimental.pallas import tpu as pltpu
from jax.sharding import PartitionSpec as P

MESH = pl.DeviceIdType.MESH
BF = jnp.bfloat16
F32 = jnp.float32
HOP = 4
NEAR = 4
RELAY = {0: (4, 3, 2, 1), 4: (4, 3, 2, 1)}


def mm(a, b):
    return jnp.dot(a, b, preferred_element_type=F32)


def nt(a, b):
    return lax.dot_general(a, b, (((1,), (1,)), ((), ())), preferred_element_type=F32)


def tn(a, b):
    return lax.dot_general(a, b, (((0,), (0,)), ((), ())), preferred_element_type=F32)


def sigmoid(v):
    return 1.0 / (1.0 + jnp.exp(-v))


def softplus(v):
    return jnp.maximum(v, 0.0) + jnp.log1p(jnp.exp(-jnp.abs(v)))


def body(
    dims,
    feat_hbm,
    w1_hbm,
    w2_hbm,
    table_hbm,
    heads_hbm,
    rels_hbm,
    tails_hbm,
    negs_hbm,
    partner_hbm,
    loss_hbm,
    pieces_hbm,
    norm_hbm,
    loss_out,
    gathered,
    norm_out,
    feat,
    w1,
    w2,
    table,
    heads,
    rels,
    tails,
    negs,
    partner,
    ids,
    buf_y,
    buf_z,
    buf_o,
    rel_rows,
    query,
    enc,
    slope,
    grads,
    dpre,
    xt,
    ht,
    core_send,
    core_recv,
    send_1,
    recv_1,
    send_2,
    recv_2,
    send_z,
    recv_z,
    parts_sq,
    squares,
    spare,
    out_sem,
    load_sem,
    send_sem,
    line_sem,
    sem_y,
    sem_z,
    sem_o,
    sem_core,
    sem_1,
    sem_2,
    sem_rz,
    sem_q,
    sem_p,
    sem_c,
    sem_s,
    sem_t,
):
    nzh, na, ng = dims
    nz = nzh * ng
    rem, div = lax.rem, lax.div
    dom = lax.axis_index("dom")
    g = lax.axis_index("grp")
    c = rem(dom, 2)
    y = rem(div(dom, 2), na)
    x = rem(div(dom, 2 * na), na)
    zh = div(dom, 2 * na * na)
    z = zh * ng + g
    bits = na.bit_length() - 1

    def dev(zh_, x_, y_, c_, g_):
        return (((zh_ * na + x_) * na + y_) * 2 + c_, g_)

    def xor(v, k):
        out = 0
        for b in range(bits):
            out = out + rem(div(v, 1 << b) + (k >> b & 1), 2) * (1 << b)
        return out

    def on_ring(step):
        to = rem(z + step + nz, nz)
        return dev(div(to, ng), x, y, c, rem(to, ng))

    other_core = dev(zh, x, y, 1 - c, g)
    conditional = []
    sent = {}

    def push(src, dst, sem, target, group):
        sent[group] = sent.get(group, 0) + 1
        pltpu.make_async_remote_copy(
            src_ref=src,
            dst_ref=dst,
            send_sem=send_sem.at[group],
            recv_sem=sem,
            device_id=target,
            device_id_type=MESH,
        ).start()

    def all_sent(group, like):
        pltpu.make_async_remote_copy(
            src_ref=like,
            dst_ref=like,
            send_sem=send_sem.at[group],
            recv_sem=sem_core.at[0],
            device_id=other_core,
            device_id_type=MESH,
        ).wait_send()

    def arrived(dst, sem):
        pltpu.make_async_remote_copy(
            src_ref=dst,
            dst_ref=dst,
            send_sem=send_sem.at[0],
            recv_sem=sem,
            device_id=other_core,
            device_id_type=MESH,
        ).wait_recv()

    def ring(buf, sem, group):
        far = nz // 2
        waited = set()
        for base in sorted(RELAY):
            for way in (1, -1):
                if base >= far:
                    continue
                source = rem(z - way * base + nz, nz)
                held, flag = buf.at[source], sem.at[source]
                if base:
                    arrived(held, flag)
                    waited.add(way * base)
                for step in RELAY[base]:
                    if base + step < far:
                        push(held, held, flag, on_ring(way * step), group)
                    elif base + step == far:
                        part = held.at[(1 - way) // 2]
                        push(part, part, flag, on_ring(way * step), group)
            yield
        for dist in range(1, far + 1):
            for way in (1, -1):
                if way * dist not in waited and (way == 1 or dist < far):
                    source = rem(z - way * dist + nz, nz)
                    arrived(buf.at[source], sem.at[source])

    def push_if(cond, *what):
        index = len(conditional)

        def make():
            src, dst, sem, target = what
            return pltpu.make_async_remote_copy(
                src_ref=src,
                dst_ref=dst,
                send_sem=line_sem.at[index],
                recv_sem=sem,
                device_id=target,
                device_id_type=MESH,
            )

        @pl.when(cond)
        def _():
            make().start()

        conditional.append((cond, make))

    def arrived_if(cond, *what):
        @pl.when(cond)
        def _():
            arrived(*what)

    def line(buf, sem):
        def within(k):
            return jnp.logical_and(k >= 0, k < ng)

        seen = set()
        for base in range(0, ng - 1, HOP):
            for way in (1, -1):
                source = g - way * base
                there = within(source)
                held = buf.at[rem(source + ng, ng)]
                flag = sem.at[rem(source + ng, ng)]
                if base:
                    arrived_if(there, held, flag)
                    seen.add(-way * base)
                for step in range(min(HOP, ng - 1 - base), 0, -1):
                    to = g + way * step
                    both = jnp.logical_and(there, within(to))
                    push_if(both, held, held, flag, dev(zh, x, y, c, rem(to + ng, ng)))
            yield
        for way in (1, -1):
            for dist in range(1, ng):
                if -way * dist not in seen:
                    source = rem(g - way * dist + ng, ng)
                    arrived_if(within(g - way * dist), buf.at[source], sem.at[source])

    barrier = pltpu.get_barrier_semaphore()
    places = na * na
    shifts = sorted(range(1, 2 * places), key=lambda k: -sum(min(v, na - v) for v in (k // (2 * na), k // 2 % na)))

    def shifted(k):
        return dev(zh, xor(x, k // (2 * na)), xor(y, k // 2 % na), rem(c + k % 2, 2), g)

    peers = [shifted(k) for k in shifts]
    near = min(NEAR, nz // 2)
    peers += [on_ring(k) for k in range(1, nz) if min(k, nz - k) <= near]
    for peer in peers:
        pl.semaphore_signal(barrier, inc=1, device_id=peer, device_id_type=MESH)

    pairs = (
        (feat_hbm, feat),
        (feat_hbm, buf_y.at[0]),
        (feat_hbm, buf_o.at[g]),
        (partner_hbm, partner),
        (heads_hbm, heads),
        (rels_hbm, rels),
        (tails_hbm, tails),
        (negs_hbm, negs),
        (table_hbm, table),
        (w1_hbm, w1),
        (w2_hbm, w2),
    )
    loads = []
    for i, (src, dst) in enumerate(pairs):
        loads.append(pltpu.make_async_copy(src, dst, load_sem.at[i]))
        loads[-1].start()
    for load in loads[0:3]:
        load.wait()
    pl.semaphore_wait(barrier, len(peers))

    for k in shifts:
        push(feat, buf_y.at[k], sem_y.at[0], shifted(k), 0)
    own_ring = line(buf_o, sem_o)
    next(own_ring)

    for load in loads[3:9]:
        load.wait()
    ids[0:2] = heads[...].astype(F32)
    ids[2:4] = rels[...].astype(F32)
    ids[4:6] = tails[...].astype(F32)
    ids[6:8] = jnp.zeros_like(ids[6:8])
    columns = jnp.transpose(ids[...])
    nrel = table.shape[0]
    edges = heads.shape[1]
    for r in range(2):
        pick = lax.broadcasted_iota(jnp.int32, (edges, nrel), 1).astype(F32) == columns[:, 2 + r : 3 + r]
        rel_rows[r] = mm(pick.astype(BF), table[...]).astype(BF)

    masks = [partner[r, 0] for r in range(2)]
    next(own_ring, None)
    arrived(buf_y.at[pl.ds(1, 2 * places - 1)], sem_y.at[0])
    for r in range(2):
        buf_z[z, r] = buf_y[masks[r] % (2 * places)]
    far_ring = ring(buf_z, sem_z, 2)
    next(far_ring)
    next(far_ring)
    for _ in own_ring:
        pass

    for load in loads[9:]:
        load.wait()
    rows = 8 * ng
    half = w2.shape[1] // 2
    lane = lax.broadcasted_iota(jnp.int32, (edges, rows), 1).astype(F32)

    def encode(x_rows, first, count, at):
        pre = mm(x_rows, w1[...])
        s = sigmoid(pre)
        hidden = (pre * s).astype(BF)
        enc[first : first + count] = mm(hidden, w2[...]).astype(BF)
        slope[first : first + count] = s * (1.0 + pre * (1.0 - s))
        xt[:, at : at + count] = jnp.transpose(x_rows)
        ht[:, at : at + count] = jnp.transpose(hidden)

    own_x = buf_o[...].astype(F32).reshape(rows, feat.shape[1]).astype(BF)
    encode(own_x, 2 * rows, rows, 2 * rows)
    picks = []
    for r in range(2):
        head_pick = (lane == columns[:, r : r + 1]).astype(BF)
        picks.append(head_pick)
        head = mm(head_pick, enc[2 * rows : 3 * rows])
        rel = rel_rows[r].astype(F32)
        h_re, h_im = head[:, :half], head[:, half:]
        r_re, r_im = rel[:, :half], rel[:, half:]
        query[r, :, :half] = (h_re * r_re - h_im * r_im).astype(BF)
        query[r, :, half:] = (h_re * r_im + h_im * r_re).astype(BF)
    counts = []
    nneg = negs.shape[1]
    for r in range(2):
        hit = lax.broadcasted_iota(jnp.int32, (rows, nneg), 0) == negs[r : r + 1, :]
        counts.append(nt(jnp.ones((8, nneg), BF), hit.astype(F32).astype(BF))[0:1])
    for _ in far_ring:
        pass

    far = []
    for r in range(2):
        half_of = rem(zh + (masks[r] // (2 * places)) % 2, 2)
        rows_r = buf_z[pl.ds(half_of * ng, ng), r]
        far.append(rows_r.astype(F32).reshape(rows, feat.shape[1]))
    encode(jnp.concatenate(far, axis=0).astype(BF), 0, 2 * rows, 0)

    own = None
    losses = []
    for r in range(2):
        other = enc[r * rows : (r + 1) * rows]
        q = query[r]
        score = nt(q, other)
        tail_pick = jnp.where(lane == columns[:, 4 + r : 5 + r], 1.0, 0.0)
        positive = jnp.sum(score * tail_pick, axis=1, keepdims=True)
        losses.append(
            softplus(-positive) + jnp.sum(softplus(score) * counts[r], axis=1, keepdims=True) / nneg
        )
        weight_neg = (sigmoid(score) / nneg).astype(BF).astype(F32)
        weight_pos = -sigmoid(-positive)
        weight = (weight_neg * counts[r] + tail_pick * weight_pos).astype(BF)
        d_query = mm(weight, other)
        grads[r * rows : (r + 1) * rows] = tn(weight, q).astype(BF)
        rel = rel_rows[r].astype(F32)
        q_re, q_im = d_query[:, :half], d_query[:, half:]
        r_re, r_im = rel[:, :half], rel[:, half:]
        d_head = jnp.concatenate([q_re * r_re + q_im * r_im, q_im * r_re - q_re * r_im], axis=1)
        term = tn(picks[r], d_head.astype(BF))
        own = term if own is None else own + term
    grads[2 * rows : 3 * rows] = own.astype(BF)
    wide = lax.broadcasted_iota(jnp.int32, (edges, 128), 1)
    both = jnp.where(wide == 0, losses[0], jnp.where(wide == 1, losses[1], 0.0))
    loss_out[...] = jnp.transpose(both)[0:2]
    outs = [
        pltpu.make_async_copy(loss_out, loss_hbm, out_sem.at[0]),
        pltpu.make_async_copy(gathered, pieces_hbm, out_sem.at[1]),
        pltpu.make_async_copy(norm_out, norm_hbm, out_sem.at[2]),
    ]
    outs[0].start()

    dpre[...] = (nt(grads[...], w2[...]) * slope[...]).astype(BF)
    rows_1, rows_2 = w1.shape[0] // ng, w2.shape[0] // ng
    part_1, part_w2 = rows_1 // na, rows_2 // na
    block = part_1 + part_w2
    width = w2.shape[1] // na
    halves = ng // 2

    def slice_of(which, put):
        first_1 = pl.multiple_of(which * rows_1, rows_1)
        first_2 = pl.multiple_of(which * rows_2, rows_2)
        t1 = mm(xt[pl.ds(first_1, rows_1), 0 : 3 * rows], dpre[...])
        t2 = mm(ht[pl.ds(first_2, rows_2), 0 : 3 * rows], grads[...])
        for i in range(na):
            put(i, t2[i * part_w2 : (i + 1) * part_w2], t1[i * part_1 : (i + 1) * part_1])

    for gh in range(halves):

        def put_send(i, low, high, gh=gh):
            core_send[gh, i, 0:part_w2] = low.astype(BF)
            core_send[gh, i, part_w2:block] = high.astype(BF)

        slice_of(2 * gh + 1 - c, put_send)
        push(core_send.at[gh], core_recv.at[gh], sem_core.at[gh], other_core, 3)
    a = c * x + (1 - c) * y
    b = c * y + (1 - c) * x
    slot = a * na + b
    ways = sorted(range(1, places), key=lambda k: -sum(min(v, na - v) for v in (k // na, k % na)))

    def in_plane(k):
        ka, kb = div(k, na), rem(k, na)
        return dev(zh, c * ka + (1 - c) * kb, c * kb + (1 - c) * ka, c, g)

    def turned(k):
        return rem(a + k // na, na) * na + rem(b + k % na, na)

    def along_a(k):
        return dev(zh, c * k + (1 - c) * x, c * y + (1 - c) * k, c, g)

    def along_b(k):
        return dev(zh, c * x + (1 - c) * k, c * k + (1 - c) * y, c, g)

    steps = sorted(range(1, na), key=lambda k: -min(k, na - k))
    for gh in range(halves):
        local = []
        slice_of(2 * gh + c, lambda i, low, high: local.append((low, high)))
        arrived(core_recv.at[gh], sem_core.at[gh])
        for i, (low, high) in enumerate(local):
            low = low + core_recv[gh, i, 0:part_w2].astype(F32)
            high = high + core_recv[gh, i, part_w2:block].astype(F32)
            send_1[gh, i, 0:part_w2] = low.astype(BF)
            send_1[gh, i, part_w2:block] = high.astype(BF)
        for j in steps:
            k = rem(a + j, na)
            push(send_1.at[gh, k], recv_1.at[gh, a], sem_1.at[gh], along_a(k), 4)
    for gh in range(halves):
        arrived(recv_1.at[gh, pl.ds(0, na - 1)], sem_1.at[gh])
        part = send_1[gh, a].astype(F32)
        for j in range(1, na):
            part = part + recv_1[gh, rem(a + j, na)].astype(F32)
        for k in range(na):
            send_2[gh, k] = part[:, k * width : (k + 1) * width].astype(BF)
        for j in steps:
            k = rem(b + j, na)
            push(send_2.at[gh, k], recv_2.at[gh, b], sem_2.at[gh], along_b(k), 5)
    matched = rem(g + c, 2) == 0
    for gh in range(halves):
        arrived(recv_2.at[gh, pl.ds(0, na - 1)], sem_2.at[gh])
        part = send_2[gh, b].astype(F32)
        for j in range(1, na):
            part = part + recv_2[gh, rem(b + j, na)].astype(F32)
        send_z[gh] = part.astype(BF)
        to = 2 * gh + c
        for zp in range(nzh):
            to_z = rem(zh + zp, nzh)
            elsewhere = jnp.logical_or(to_z != zh, to != g)
            target = dev(to_z, x, y, c, to)

            @pl.when(elsewhere)
            def _(gh=gh, target=target):
                push(send_z.at[gh], recv_z.at[z], sem_rz.at[0], target, 6)


    @pl.when(matched)
    def _():
        recv_z[z] = send_z[div(g, 2)]
        arrived(recv_z.at[pl.ds(0, nz - 1)], sem_rz.at[0])
        piece = jnp.zeros((block, width), F32)
        for k in range(nz):
            piece = piece + recv_z[k].astype(F32)
        squares[g] = jnp.full((1, width), jnp.sum(piece * piece), F32)
        for k in sorted(range(1 - ng // 2, ng // 2 + 1), key=abs, reverse=True):
            if k:
                to = rem(z + k + nz, nz)
                target = dev(div(to, ng), x, y, rem(c + k + nz, 2), rem(to, ng))
                push(squares.at[g], squares.at[g], sem_s.at[0], target, 7)
        gathered[slot] = piece.astype(BF)
        for k in ways:
            push(gathered.at[slot], gathered.at[slot], sem_p.at[0], in_plane(turned(k)), 8)
        arrived(squares.at[pl.ds(0, ng - 1)], sem_s.at[0])
        ss = squares[0]
        for k in range(1, ng):
            ss = ss + squares[k]
        parts_sq[slot] = ss
        for k in ways:
            for cc in range(2):
                ka, kb = div(turned(k), na), rem(turned(k), na)
                target = dev(zh, c * ka + (1 - c) * kb, c * kb + (1 - c) * ka, cc, g)
                push(parts_sq.at[slot], parts_sq.at[slot], sem_q.at[0], target, 9)
        push(parts_sq.at[slot], parts_sq.at[slot], sem_t.at[0], other_core, 10)
        arrived(gathered.at[pl.ds(0, places - 1)], sem_p.at[0])
        push(gathered, gathered, sem_c.at[0], other_core, 11)
        outs[1].start()
        all_sent(7, squares.at[pl.ds(0, ng - 1)])
        all_sent(8, gathered.at[pl.ds(0, places - 1)])
        all_sent(9, spare)
        all_sent(10, parts_sq.at[0])
        all_sent(11, gathered)
        all_sent(6, recv_z.at[pl.ds(0, halves * nzh - 1)])

    @pl.when(jnp.logical_not(matched))
    def _():
        arrived(parts_sq.at[0], sem_t.at[0])
        arrived(gathered, sem_c.at[0])
        outs[1].start()
        all_sent(6, recv_z.at[pl.ds(0, halves * nzh)])

    arrived(parts_sq.at[pl.ds(0, places - 1)], sem_q.at[0])
    ss = parts_sq[0]
    for k in range(1, places):
        ss = ss + parts_sq[k]
    norm_out[...] = ss
    outs[2].start()

    all_sent(0, buf_y.at[pl.ds(1, 2 * places - 1)])
    all_sent(2, buf_z.at[pl.ds(0, nz - 1)])
    all_sent(3, core_send)
    all_sent(4, send_1.at[pl.ds(0, halves), pl.ds(0, na - 1)])
    all_sent(5, send_2.at[pl.ds(0, halves), pl.ds(0, na - 1)])
    for cond, make in conditional:

        @pl.when(cond)
        def _(make=make):
            make().wait_send()

    for copy in outs:
        copy.wait()


def finish(na, count, loss_in, pieces, squares, loss_out, g1_out, g2_out):
    low = g2_out.shape[0] // na
    high = g1_out.shape[0] // na
    width = pieces.shape[2]
    factor = jnp.minimum(1.0, math.sqrt(count) / jnp.sqrt(squares[...] + 1e-06))
    loss_out[...] = loss_in[...]
    for i in range(na):
        for k in range(na):
            column = slice(k * width, (k + 1) * width)
            g2_out[i * low : (i + 1) * low, column] = pieces[i * na + k, 0:low].astype(F32) * factor
            g1_out[i * high : (i + 1) * high, column] = pieces[i * na + k, low:].astype(F32) * factor


def per_device(dims, features, w_first, w_second, table, heads, relations, tails, negatives, partner):
    nzh, na, ng = dims
    nz = nzh * ng
    own, d_in = features.shape
    d_hid, d_enc = w_second.shape
    edges = heads.shape[1]
    rows = own * ng
    rows_1, rows_2 = d_in // ng, d_hid // ng
    block, width, halves = (rows_1 + rows_2) // na, d_enc // na, ng // 2
    lanes = max(256, 3 * rows)
    vmem = pl.BlockSpec(memory_space=pltpu.VMEM)
    hbm = pl.BlockSpec(memory_space=pltpu.HBM)
    V, S = pltpu.VMEM, pltpu.SemaphoreType.DMA
    loss, pieces, squares = pl.pallas_call(
        functools.partial(body, dims),
        out_shape=(
            jax.ShapeDtypeStruct(heads.shape, F32),
            jax.ShapeDtypeStruct((na * na, block, width), BF),
            jax.ShapeDtypeStruct((1, width), F32),
        ),
        in_specs=[hbm] * 9,
        out_specs=(hbm, hbm, hbm),
        scratch_shapes=[
            V(heads.shape, F32),
            V((na * na, block, width), BF),
            V((1, width), F32),
            V(features.shape, BF),
            V(w_first.shape, BF),
            V(w_second.shape, BF),
            V(table.shape, BF),
            V(heads.shape, jnp.int32),
            V(relations.shape, jnp.int32),
            V(tails.shape, jnp.int32),
            V(negatives.shape, jnp.int32),
            pltpu.SMEM(partner.shape, jnp.int32),
            V((8, edges), F32),
            V((2 * na * na, own, d_in), BF),
            V((nz, 2, own, d_in), BF),
            V((ng, own, d_in), BF),
            V((2, edges, d_enc), BF),
            V((2, edges, d_enc), BF),
            V((3 * rows, d_enc), BF),
            V((3 * rows, d_hid), F32),
            V((3 * rows, d_enc), BF),
            V((3 * rows, d_hid), BF),
            V((d_in, lanes), BF),
            V((d_hid, lanes), BF),
            V((halves, na, block, d_enc), BF),
            V((halves, na, block, d_enc), BF),
            V((halves, na, block, d_enc), BF),
            V((halves, na, block, d_enc), BF),
            V((halves, na, block, width), BF),
            V((halves, na, block, width), BF),
            V((halves, block, width), BF),
            V((nz, block, width), BF),
            V((na * na, 1, width), F32),
            V((ng, 1, width), F32),
            V((2 * na * na - 2, 1, width), F32),
            S((3,)),
            S((11,)),
            S((12,)),
            S((14,)),
            S((1,)),
            S((nz,)),
            S((ng,)),
            S((halves,)),
            S((halves,)),
            S((halves,)),
            S((1,)),
            S((1,)),
            S((1,)),
            S((1,)),
            S((1,)),
            S((1,)),
        ],
        compiler_params=pltpu.CompilerParams(
            collective_id=0, has_side_effects=True, vmem_limit_bytes=60 * 1024 * 1024
        ),
        name="step",
    )(features, w_first, w_second, table, heads, relations, tails, negatives, partner)
    return pl.pallas_call(
        functools.partial(finish, na, float(w_first.size + w_second.size)),
        out_shape=(
            jax.ShapeDtypeStruct(heads.shape, F32),
            jax.ShapeDtypeStruct((rows_1, d_hid), F32),
            jax.ShapeDtypeStruct((rows_2, d_enc), F32),
        ),
        in_specs=[vmem] * 3,
        out_specs=(vmem, vmem, vmem),
        name="finish",
    )(loss, pieces, squares)


def solution(mesh):
    ng = mesh.shape["grp"]
    na = math.isqrt(mesh.shape["dom"] // 4)
    return jax.shard_map(
        functools.partial(per_device, (2, na, ng)),
        mesh=mesh,
        in_specs=(
            P(("dom", "grp"), None),
            P(),
            P(),
            P(),
            P(None, ("dom", "grp")),
            P(None, ("dom", "grp")),
            P(None, ("dom", "grp")),
            P(),
            P(),
        ),
        out_specs=(P(None, ("dom", "grp")), P("grp", None), P("grp", None)),
        check_vma=False,
    )
```

```python
import functools
import math

import jax
import jax.numpy as jnp
from jax import lax
from jax.experimental import pallas as pl
from jax.experimental.pallas import tpu as pltpu
from jax.sharding import PartitionSpec as P

MESH = pl.DeviceIdType.MESH
BF = jnp.bfloat16
F32 = jnp.float32
HOP = 4
NEAR = 4
STEP = 1
RELAY = {0: (4, 3, 2, 1), 4: (4, 3, 2, 1)}


def mm(a, b):
    return jnp.dot(a, b, preferred_element_type=F32)


def nt(a, b):
    return lax.dot_general(a, b, (((1,), (1,)), ((), ())), preferred_element_type=F32)


def tn(a, b):
    return lax.dot_general(a, b, (((0,), (0,)), ((), ())), preferred_element_type=F32)


def sigmoid(v):
    return 1.0 / (1.0 + jnp.exp(-v))


def softplus(v):
    return jnp.maximum(v, 0.0) + jnp.log1p(jnp.exp(-jnp.abs(v)))


def body(
    dims,
    feat_hbm,
    w1_hbm,
    w2_hbm,
    table_hbm,
    heads_hbm,
    rels_hbm,
    tails_hbm,
    negs_hbm,
    partner_hbm,
    loss_hbm,
    pieces_hbm,
    norm_hbm,
    loss_out,
    gathered,
    norm_out,
    feat,
    w1,
    w2,
    table,
    heads,
    rels,
    tails,
    negs,
    partner,
    ids,
    buf_y,
    buf_z,
    buf_o,
    rel_rows,
    query,
    enc,
    slope,
    grads,
    dpre,
    xt,
    ht,
    core_send,
    core_recv,
    send_1,
    recv_1,
    send_z,
    recv_z,
    parts_sq,
    squares,
    spare,
    out_sem,
    load_sem,
    send_sem,
    line_sem,
    sem_y,
    sem_z,
    sem_o,
    sem_core,
    sem_1,
    sem_rz,
    sem_q,
    sem_p,
    sem_c,
    sem_s,
    sem_t,
):
    nzh, na, ng = dims
    nz = nzh * ng
    rem, div = lax.rem, lax.div
    dom = lax.axis_index("dom")
    g = lax.axis_index("grp")
    c = rem(dom, 2)
    y = rem(div(dom, 2), na)
    x = rem(div(dom, 2 * na), na)
    zh = div(dom, 2 * na * na)
    z = zh * ng + g
    bits = na.bit_length() - 1

    def dev(zh_, x_, y_, c_, g_):
        return (((zh_ * na + x_) * na + y_) * 2 + c_, g_)

    def xor(v, k):
        out = 0
        for b in range(bits):
            out = out + rem(div(v, 1 << b) + (k >> b & 1), 2) * (1 << b)
        return out

    def on_ring(step):
        to = rem(z + step + nz, nz)
        return dev(div(to, ng), x, y, c, rem(to, ng))

    other_core = dev(zh, x, y, 1 - c, g)
    conditional = []
    sent = {}

    def push(src, dst, sem, target, group):
        sent[group] = sent.get(group, 0) + 1
        pltpu.make_async_remote_copy(
            src_ref=src,
            dst_ref=dst,
            send_sem=send_sem.at[group],
            recv_sem=sem,
            device_id=target,
            device_id_type=MESH,
        ).start()

    def all_sent(group, like):
        pltpu.make_async_remote_copy(
            src_ref=like,
            dst_ref=like,
            send_sem=send_sem.at[group],
            recv_sem=sem_core.at[0],
            device_id=other_core,
            device_id_type=MESH,
        ).wait_send()

    def arrived(dst, sem):
        pltpu.make_async_remote_copy(
            src_ref=dst,
            dst_ref=dst,
            send_sem=send_sem.at[0],
            recv_sem=sem,
            device_id=other_core,
            device_id_type=MESH,
        ).wait_recv()

    def ring(buf, sem, group):
        far = nz // 2
        waited = set()
        for base in sorted(RELAY):
            for way in (1, -1):
                if base >= far:
                    continue
                source = rem(z - way * base + nz, nz)
                held, flag = buf.at[source], sem.at[source]
                if base:
                    arrived(held, flag)
                    waited.add(way * base)
                for step in RELAY[base]:
                    if base + step < far:
                        push(held, held, flag, on_ring(way * step), group)
                    elif base + step == far:
                        part = held.at[(1 - way) // 2]
                        push(part, part, flag, on_ring(way * step), group)
            yield
        for dist in range(1, far + 1):
            for way in (1, -1):
                if way * dist not in waited and (way == 1 or dist < far):
                    source = rem(z - way * dist + nz, nz)
                    arrived(buf.at[source], sem.at[source])

    def push_if(cond, *what):
        index = len(conditional)

        def make():
            src, dst, sem, target = what
            return pltpu.make_async_remote_copy(
                src_ref=src,
                dst_ref=dst,
                send_sem=line_sem.at[index],
                recv_sem=sem,
                device_id=target,
                device_id_type=MESH,
            )

        @pl.when(cond)
        def _():
            make().start()

        conditional.append((cond, make))

    def arrived_if(cond, *what):
        @pl.when(cond)
        def _():
            arrived(*what)

    def line(buf, sem):
        def within(k):
            return jnp.logical_and(k >= 0, k < ng)

        seen = set()
        for base in range(0, ng - 1, HOP):
            for way in (1, -1):
                source = g - way * base
                there = within(source)
                held = buf.at[rem(source + ng, ng)]
                flag = sem.at[rem(source + ng, ng)]
                if base:
                    arrived_if(there, held, flag)
                    seen.add(-way * base)
                for step in range(min(HOP, ng - 1 - base), 0, -1):
                    to = g + way * step
                    both = jnp.logical_and(there, within(to))
                    push_if(both, held, held, flag, dev(zh, x, y, c, rem(to + ng, ng)))
            yield
        for way in (1, -1):
            for dist in range(1, ng):
                if -way * dist not in seen:
                    source = rem(g - way * dist + ng, ng)
                    arrived_if(within(g - way * dist), buf.at[source], sem.at[source])

    barrier = pltpu.get_barrier_semaphore()
    places = na * na
    shifts = sorted(range(1, 2 * places), key=lambda k: -sum(min(v, na - v) for v in (k // (2 * na), k // 2 % na)))

    def shifted(k):
        return dev(zh, xor(x, k // (2 * na)), xor(y, k // 2 % na), rem(c + k % 2, 2), g)

    peers = [shifted(k) for k in shifts]
    near = min(NEAR, nz // 2)
    peers += [on_ring(k) for k in range(1, nz) if min(k, nz - k) <= near]
    for peer in peers:
        pl.semaphore_signal(barrier, inc=1, device_id=peer, device_id_type=MESH)

    pairs = (
        (feat_hbm, feat),
        (feat_hbm, buf_y.at[0]),
        (feat_hbm, buf_o.at[g]),
        (partner_hbm, partner),
        (heads_hbm, heads),
        (rels_hbm, rels),
        (tails_hbm, tails),
        (negs_hbm, negs),
        (table_hbm, table),
        (w1_hbm, w1),
        (w2_hbm, w2),
    )
    loads = []
    for i, (src, dst) in enumerate(pairs):
        loads.append(pltpu.make_async_copy(src, dst, load_sem.at[i]))
        loads[-1].start()
    for load in loads[0:3]:
        load.wait()
    pl.semaphore_wait(barrier, len(peers))

    for k in shifts:
        push(feat, buf_y.at[k], sem_y.at[0], shifted(k), 0)
    own_ring = line(buf_o, sem_o)
    next(own_ring)

    for load in loads[3:9]:
        load.wait()
    ids[0:2] = heads[...].astype(F32)
    ids[2:4] = rels[...].astype(F32)
    ids[4:6] = tails[...].astype(F32)
    ids[6:8] = jnp.zeros_like(ids[6:8])
    columns = jnp.transpose(ids[...])
    nrel = table.shape[0]
    edges = heads.shape[1]
    for r in range(2):
        pick = lax.broadcasted_iota(jnp.int32, (edges, nrel), 1).astype(F32) == columns[:, 2 + r : 3 + r]
        rel_rows[r] = mm(pick.astype(BF), table[...]).astype(BF)

    masks = [partner[r, 0] for r in range(2)]
    next(own_ring, None)
    arrived(buf_y.at[pl.ds(1, 2 * places - 1)], sem_y.at[0])
    for r in range(2):
        buf_z[z, r] = buf_y[masks[r] % (2 * places)]
    far_ring = ring(buf_z, sem_z, 2)
    next(far_ring)
    next(far_ring)
    for _ in own_ring:
        pass

    for load in loads[9:]:
        load.wait()
    rows = 8 * ng
    half = w2.shape[1] // 2
    lane = lax.broadcasted_iota(jnp.int32, (edges, rows), 1).astype(F32)

    def encode(x_rows, first, count, at):
        pre = mm(x_rows, w1[...])
        s = sigmoid(pre)
        hidden = (pre * s).astype(BF)
        enc[first : first + count] = mm(hidden, w2[...]).astype(BF)
        slope[first : first + count] = s * (1.0 + pre * (1.0 - s))
        xt[:, at : at + count] = jnp.transpose(x_rows)
        ht[:, at : at + count] = jnp.transpose(hidden)

    own_x = buf_o[...].astype(F32).reshape(rows, feat.shape[1]).astype(BF)
    encode(own_x, 2 * rows, rows, 2 * rows)
    picks = []
    for r in range(2):
        head_pick = (lane == columns[:, r : r + 1]).astype(BF)
        picks.append(head_pick)
        head = mm(head_pick, enc[2 * rows : 3 * rows])
        rel = rel_rows[r].astype(F32)
        h_re, h_im = head[:, :half], head[:, half:]
        r_re, r_im = rel[:, :half], rel[:, half:]
        query[r, :, :half] = (h_re * r_re - h_im * r_im).astype(BF)
        query[r, :, half:] = (h_re * r_im + h_im * r_re).astype(BF)
    counts = []
    nneg = negs.shape[1]
    for r in range(2):
        hit = lax.broadcasted_iota(jnp.int32, (rows, nneg), 0) == negs[r : r + 1, :]
        counts.append(nt(jnp.ones((8, nneg), BF), hit.astype(F32).astype(BF))[0:1])
    for _ in far_ring:
        pass

    far = []
    for r in range(2):
        half_of = rem(zh + (masks[r] // (2 * places)) % 2, 2)
        rows_r = buf_z[pl.ds(half_of * ng, ng), r]
        far.append(rows_r.astype(F32).reshape(rows, feat.shape[1]))
    encode(jnp.concatenate(far, axis=0).astype(BF), 0, 2 * rows, 0)

    own = None
    losses = []
    for r in range(2):
        other = enc[r * rows : (r + 1) * rows]
        q = query[r]
        score = nt(q, other)
        tail_pick = jnp.where(lane == columns[:, 4 + r : 5 + r], 1.0, 0.0)
        positive = jnp.sum(score * tail_pick, axis=1, keepdims=True)
        losses.append(
            softplus(-positive) + jnp.sum(softplus(score) * counts[r], axis=1, keepdims=True) / nneg
        )
        weight_neg = (sigmoid(score) / nneg).astype(BF).astype(F32)
        weight_pos = -sigmoid(-positive)
        weight = (weight_neg * counts[r] + tail_pick * weight_pos).astype(BF)
        d_query = mm(weight, other)
        grads[r * rows : (r + 1) * rows] = tn(weight, q).astype(BF)
        rel = rel_rows[r].astype(F32)
        q_re, q_im = d_query[:, :half], d_query[:, half:]
        r_re, r_im = rel[:, :half], rel[:, half:]
        d_head = jnp.concatenate([q_re * r_re + q_im * r_im, q_im * r_re - q_re * r_im], axis=1)
        term = tn(picks[r], d_head.astype(BF))
        own = term if own is None else own + term
    grads[2 * rows : 3 * rows] = own.astype(BF)
    wide = lax.broadcasted_iota(jnp.int32, (edges, 128), 1)
    both = jnp.where(wide == 0, losses[0], jnp.where(wide == 1, losses[1], 0.0))
    loss_out[...] = jnp.transpose(both)[0:2]
    outs = [
        pltpu.make_async_copy(loss_out, loss_hbm, out_sem.at[0]),
        pltpu.make_async_copy(gathered, pieces_hbm, out_sem.at[1]),
        pltpu.make_async_copy(norm_out, norm_hbm, out_sem.at[2]),
    ]
    outs[0].start()

    dpre[...] = (nt(grads[...], w2[...]) * slope[...]).astype(BF)
    rows_1, rows_2 = w1.shape[0] // ng, w2.shape[0] // ng
    part_1, part_w2 = rows_1 // na, rows_2 // na
    block = part_1 + part_w2
    width = w2.shape[1] // na
    halves = ng // 2

    def slice_of(which, put):
        first_1 = pl.multiple_of(which * rows_1, rows_1)
        first_2 = pl.multiple_of(which * rows_2, rows_2)
        t1 = mm(xt[pl.ds(first_1, rows_1), 0 : 3 * rows], dpre[...])
        t2 = mm(ht[pl.ds(first_2, rows_2), 0 : 3 * rows], grads[...])
        for i in range(na):
            put(i, t2[i * part_w2 : (i + 1) * part_w2], t1[i * part_1 : (i + 1) * part_1])

    for gh in range(halves):

        def put_send(i, low, high, gh=gh):
            core_send[gh, i, 0:part_w2] = low.astype(BF)
            core_send[gh, i, part_w2:block] = high.astype(BF)

        slice_of(2 * gh + 1 - c, put_send)
        push(core_send.at[gh], core_recv.at[gh], sem_core.at[gh], other_core, 3)
    a = c * x + (1 - c) * y
    b = c * y + (1 - c) * x
    slot = a * na + b
    ways = sorted(range(1, places), key=lambda k: -sum(min(v, na - v) for v in (k // na, k % na)))

    def in_plane(k):
        ka, kb = div(k, na), rem(k, na)
        return dev(zh, c * ka + (1 - c) * kb, c * kb + (1 - c) * ka, c, g)

    def turned(k):
        return rem(a + k // na, na) * na + rem(b + k % na, na)

    for first in range(0, halves, STEP):
        for gh in range(first, min(first + STEP, halves)):
            local = []
            slice_of(2 * gh + c, lambda i, low, high: local.append((low, high)))
            arrived(core_recv.at[gh], sem_core.at[gh])
            for i, (low, high) in enumerate(local):
                low = (low + core_recv[gh, i, 0:part_w2].astype(F32)).astype(BF)
                high = (high + core_recv[gh, i, part_w2:block].astype(F32)).astype(BF)
                for k in range(na):
                    column = slice(k * width, (k + 1) * width)
                    send_1[i * na + k, gh, 0:part_w2] = low[:, column]
                    send_1[i * na + k, gh, part_w2:block] = high[:, column]
        some = pl.ds(first, min(STEP, halves - first))
        for k in ways:
            to = turned(k)
            push(send_1.at[to, some], recv_1.at[slot, some], sem_1.at[first], in_plane(to), 4)
        recv_1[slot, some] = send_1[slot, some]
    matched = rem(g + c, 2) == 0
    for gh in range(halves):
        if gh % STEP == 0:
            some = pl.ds(gh, min(STEP, halves - gh))
            arrived(recv_1.at[pl.ds(0, places - 1), some], sem_1.at[gh])
        part = recv_1[0, gh].astype(F32)
        for k in range(1, places):
            part = part + recv_1[k, gh].astype(F32)
        send_z[gh] = part.astype(BF)
        to = 2 * gh + c
        for zp in range(nzh):
            to_z = rem(zh + zp, nzh)
            elsewhere = jnp.logical_or(to_z != zh, to != g)
            target = dev(to_z, x, y, c, to)

            @pl.when(elsewhere)
            def _(gh=gh, target=target):
                push(send_z.at[gh], recv_z.at[z], sem_rz.at[0], target, 6)


    @pl.when(matched)
    def _():
        recv_z[z] = send_z[div(g, 2)]
        arrived(recv_z.at[pl.ds(0, nz - 1)], sem_rz.at[0])
        piece = jnp.zeros((block, width), F32)
        for k in range(nz):
            piece = piece + recv_z[k].astype(F32)
        squares[g] = jnp.full((1, width), jnp.sum(piece * piece), F32)
        for k in sorted(range(1 - ng // 2, ng // 2 + 1), key=abs, reverse=True):
            if k:
                to = rem(z + k + nz, nz)
                target = dev(div(to, ng), x, y, rem(c + k + nz, 2), rem(to, ng))
                push(squares.at[g], squares.at[g], sem_s.at[0], target, 7)
        gathered[slot] = piece.astype(BF)
        for k in ways:
            push(gathered.at[slot], gathered.at[slot], sem_p.at[0], in_plane(turned(k)), 8)
        arrived(squares.at[pl.ds(0, ng - 1)], sem_s.at[0])
        ss = squares[0]
        for k in range(1, ng):
            ss = ss + squares[k]
        parts_sq[slot] = ss
        for k in ways:
            for cc in range(2):
                ka, kb = div(turned(k), na), rem(turned(k), na)
                target = dev(zh, c * ka + (1 - c) * kb, c * kb + (1 - c) * ka, cc, g)
                push(parts_sq.at[slot], parts_sq.at[slot], sem_q.at[0], target, 9)
        push(parts_sq.at[slot], parts_sq.at[slot], sem_t.at[0], other_core, 10)
        arrived(gathered.at[pl.ds(0, places - 1)], sem_p.at[0])
        push(gathered, gathered, sem_c.at[0], other_core, 11)
        outs[1].start()
        all_sent(7, squares.at[pl.ds(0, ng - 1)])
        all_sent(8, gathered.at[pl.ds(0, places - 1)])
        all_sent(9, spare)
        all_sent(10, parts_sq.at[0])
        all_sent(11, gathered)
        all_sent(6, recv_z.at[pl.ds(0, halves * nzh - 1)])

    @pl.when(jnp.logical_not(matched))
    def _():
        arrived(parts_sq.at[0], sem_t.at[0])
        arrived(gathered, sem_c.at[0])
        outs[1].start()
        all_sent(6, recv_z.at[pl.ds(0, halves * nzh)])

    arrived(parts_sq.at[pl.ds(0, places - 1)], sem_q.at[0])
    ss = parts_sq[0]
    for k in range(1, places):
        ss = ss + parts_sq[k]
    norm_out[...] = ss
    outs[2].start()

    all_sent(0, buf_y.at[pl.ds(1, 2 * places - 1)])
    all_sent(2, buf_z.at[pl.ds(0, nz - 1)])
    all_sent(3, core_send)
    all_sent(4, send_1.at[pl.ds(0, places - 1)])
    for cond, make in conditional:

        @pl.when(cond)
        def _(make=make):
            make().wait_send()

    for copy in outs:
        copy.wait()


def finish(na, count, loss_in, pieces, squares, loss_out, g1_out, g2_out):
    low = g2_out.shape[0] // na
    high = g1_out.shape[0] // na
    width = pieces.shape[2]
    factor = jnp.minimum(1.0, math.sqrt(count) / jnp.sqrt(squares[...] + 1e-06))
    loss_out[...] = loss_in[...]
    for i in range(na):
        for k in range(na):
            column = slice(k * width, (k + 1) * width)
            g2_out[i * low : (i + 1) * low, column] = pieces[i * na + k, 0:low].astype(F32) * factor
            g1_out[i * high : (i + 1) * high, column] = pieces[i * na + k, low:].astype(F32) * factor


def per_device(dims, features, w_first, w_second, table, heads, relations, tails, negatives, partner):
    nzh, na, ng = dims
    nz = nzh * ng
    own, d_in = features.shape
    d_hid, d_enc = w_second.shape
    edges = heads.shape[1]
    rows = own * ng
    rows_1, rows_2 = d_in // ng, d_hid // ng
    block, width, halves = (rows_1 + rows_2) // na, d_enc // na, ng // 2
    lanes = max(256, 3 * rows)
    vmem = pl.BlockSpec(memory_space=pltpu.VMEM)
    hbm = pl.BlockSpec(memory_space=pltpu.HBM)
    V, S = pltpu.VMEM, pltpu.SemaphoreType.DMA
    loss, pieces, squares = pl.pallas_call(
        functools.partial(body, dims),
        out_shape=(
            jax.ShapeDtypeStruct(heads.shape, F32),
            jax.ShapeDtypeStruct((na * na, block, width), BF),
            jax.ShapeDtypeStruct((1, width), F32),
        ),
        in_specs=[hbm] * 9,
        out_specs=(hbm, hbm, hbm),
        scratch_shapes=[
            V(heads.shape, F32),
            V((na * na, block, width), BF),
            V((1, width), F32),
            V(features.shape, BF),
            V(w_first.shape, BF),
            V(w_second.shape, BF),
            V(table.shape, BF),
            V(heads.shape, jnp.int32),
            V(relations.shape, jnp.int32),
            V(tails.shape, jnp.int32),
            V(negatives.shape, jnp.int32),
            pltpu.SMEM(partner.shape, jnp.int32),
            V((8, edges), F32),
            V((2 * na * na, own, d_in), BF),
            V((nz, 2, own, d_in), BF),
            V((ng, own, d_in), BF),
            V((2, edges, d_enc), BF),
            V((2, edges, d_enc), BF),
            V((3 * rows, d_enc), BF),
            V((3 * rows, d_hid), F32),
            V((3 * rows, d_enc), BF),
            V((3 * rows, d_hid), BF),
            V((d_in, lanes), BF),
            V((d_hid, lanes), BF),
            V((halves, na, block, d_enc), BF),
            V((halves, na, block, d_enc), BF),
            V((na * na, halves, block, width), BF),
            V((na * na, halves, block, width), BF),
            V((halves, block, width), BF),
            V((nz, block, width), BF),
            V((na * na, 1, width), F32),
            V((ng, 1, width), F32),
            V((2 * na * na - 2, 1, width), F32),
            S((3,)),
            S((11,)),
            S((12,)),
            S((14,)),
            S((1,)),
            S((nz,)),
            S((ng,)),
            S((halves,)),
            S((halves,)),
            S((1,)),
            S((1,)),
            S((1,)),
            S((1,)),
            S((1,)),
            S((1,)),
        ],
        compiler_params=pltpu.CompilerParams(
            collective_id=0, has_side_effects=True, vmem_limit_bytes=60 * 1024 * 1024
        ),
        name="step",
    )(features, w_first, w_second, table, heads, relations, tails, negatives, partner)
    return pl.pallas_call(
        functools.partial(finish, na, float(w_first.size + w_second.size)),
        out_shape=(
            jax.ShapeDtypeStruct(heads.shape, F32),
            jax.ShapeDtypeStruct((rows_1, d_hid), F32),
            jax.ShapeDtypeStruct((rows_2, d_enc), F32),
        ),
        in_specs=[vmem] * 3,
        out_specs=(vmem, vmem, vmem),
        name="finish",
    )(loss, pieces, squares)


def solution(mesh):
    ng = mesh.shape["grp"]
    na = math.isqrt(mesh.shape["dom"] // 4)
    return jax.shard_map(
        functools.partial(per_device, (2, na, ng)),
        mesh=mesh,
        in_specs=(
            P(("dom", "grp"), None),
            P(),
            P(),
            P(),
            P(None, ("dom", "grp")),
            P(None, ("dom", "grp")),
            P(None, ("dom", "grp")),
            P(),
            P(),
        ),
        out_specs=(P(None, ("dom", "grp")), P("grp", None), P("grp", None)),
        check_vma=False,
    )
```
